32 devices in a mesh: groups: 2 (over y), chan: 4 (over z), seg: 2 (over x), freq: 2 (over core).
Axes of the slice: x: 2, y: 2, z: 4, core: 2. Of those that a mesh axis runs over, the one named last changes fastest.
Arguments:
- traces: bfloat16 [10, 1024, 4096], P('seg', ('groups', 'chan')), parts along dimension 1, may hold values from -120 to 120
- dead_mask: int32 [1024], P(('groups', 'chan')), parts along dimension 0, may hold values 0 or 1
- seg_counts: int32 [1024], P(('groups', 'chan')), parts along dimension 0, may hold values from 1 to 10
- offsets: int32 [4], replicated, may hold values from 1 to 128, as said below
Outputs:
- correlations: float32 [1024, 4, 512], P(('groups', 'chan', 'seg'), None, 'freq'), parts along dimension 0
The draws below stay inside these ranges and needn't reach their ends.
There are 2 independent parts, one for each index of `groups`. The reference program is written for one: setup_inputs(seed, part) draws one part's arguments, and reference() takes and returns one part's arrays. A program takes and returns all parts, laid end to end along the dimension named above; an argument that names none is the same for every part. Nothing has to cross between parts.
Inputs may be any that keep to these rules, and one draw needn't show every extreme that they name: The 4 offsets are distinct and one of them equals 128.
All inputs are finite; a program needn't handle non-finite values. No bound on the sum of `dead_mask` on one device may be relied on, other than what follows from the above.
Results may differ from the reference program's by a relative error of at most 0.0056.
Values may be sent and summed in bfloat16 or wider, within the bound.
A program may use at most 128 MiB of HBM per device.

```python
import math
import jax
import jax.numpy as jnp
from jax import lax

L = 4096
HALF = 32
LAGS = 512
K = 4
F = 2048
BAND = 128
C = 512
SEGS = 10


def draw_traces(key, part):
    gain_key, tap_key, noise_key = jax.random.split(key, 3)
    gains = jnp.exp(jax.random.uniform(gain_key, (1, C, 1), jnp.float32, 0.0, 2.302585))
    taps = jax.random.uniform(tap_key, (3, 1, C, 1), jnp.float32, -1.0, 1.0)
    tap_one = 0.9 * taps[0]
    tap_two = 0.6 * taps[1]
    tap_three = 0.3 * taps[2]
    noise = jnp.clip(jax.random.normal(noise_key, (SEGS, C, L + 3), jnp.float32), -4.0, 4.0)
    filtered = noise[:, :, 3:] + tap_one * noise[:, :, 2:-1] + tap_two * noise[:, :, 1:-2] + tap_three * noise[:, :, :-3]
    return (gains * filtered).astype(jnp.bfloat16)


def draw_offsets(key, part):
    chosen = jax.random.permutation(jax.random.fold_in(key, 11), BAND - 1)[:K - 1] + 1
    values = jnp.concatenate([chosen.astype(jnp.int32), jnp.full((1,), BAND, jnp.int32)])
    order = jax.random.permutation(jax.random.fold_in(key, 12), K)
    return values[order].astype(jnp.int32)


def place_ends(entries, rng, low, high):
    dims = entries.shape
    spot = [jax.random.randint(jax.random.fold_in(rng, axis), (), 0, dims[axis]) for axis in range(len(dims))]
    entries = entries.at[tuple(spot)].set(low)
    longest = dims.index(max(dims))
    spot[longest] = (spot[longest] + 1) % dims[longest]
    return entries.at[tuple(spot)].set(high)


def setup_inputs(seed: int = 0, part: int = 0) -> dict:
    streams_of = jax.random.split(jax.random.key(seed), 5)
    part_splits = jax.random.split(jax.random.fold_in(streams_of[4], part), 5)
    traces = draw_traces(jax.random.fold_in(jax.random.fold_in(streams_of[4], part), 71), part)
    dead_mask = place_ends((jax.random.randint(part_splits[1], (C,), 0, 8) < 7).astype(jnp.int32), jax.random.fold_in(part_splits[1], 1), 0, 1)
    seg_counts = place_ends(jax.random.randint(part_splits[2], (C,), 1, SEGS + 1), jax.random.fold_in(part_splits[2], 1), 1, SEGS).astype(jnp.int32)
    offsets = draw_offsets(jax.random.fold_in(streams_of[4], 71), part)
    return {"traces": traces, "dead_mask": dead_mask, "seg_counts": seg_counts, "offsets": offsets}


epsilon = 1e-06

def fourier_table(bin_first, bin_number, length):
    samples = jnp.arange(length, dtype=jnp.int32)[:, None]
    bin_index = bin_first + jnp.arange(bin_number, dtype=jnp.int32)[None, :]
    phases = (samples * bin_index % length).astype(jnp.float32) * (2.0 * math.pi / length)
    return jnp.concatenate([jnp.cos(phases), -jnp.sin(phases)], axis=1).astype(jnp.bfloat16)

def delay_table(bin_first, bin_number, length, lag_number, bin_total):
    bin_index = bin_first + jnp.arange(bin_number, dtype=jnp.int32)[:, None]
    shifts = jnp.arange(lag_number, dtype=jnp.int32)[None, :] - lag_number // 2
    phases = (bin_index * shifts % length).astype(jnp.float32) * (2.0 * math.pi / length)
    scaling = 1.0 / math.sqrt(bin_total)
    return jnp.concatenate([jnp.cos(phases) * scaling, -jnp.sin(phases) * scaling], axis=0)

def reference(traces, dead_mask, seg_counts, offsets):
    fourier = fourier_table(0, F, L).astype(jnp.float32)
    bin_index = jnp.arange(F, dtype=jnp.int32)
    window_count = (jnp.minimum(bin_index + HALF, F - 1) - jnp.maximum(bin_index - HALF, 0) + 1).astype(jnp.float32)
    alive = dead_mask.astype(jnp.float32)
    zero_rows = jnp.zeros((BAND, F), jnp.float32)

    def segment(stacked, inputs):
        samples, seg_number = inputs
        spectra = jnp.dot(samples.astype(jnp.float32), fourier, precision=lax.Precision.HIGHEST)
        real_part = spectra[:, :F]
        imag_part = spectra[:, F:]
        power_bins = real_part * real_part + imag_part * imag_part
        window_sum = lax.reduce_window(power_bins, jnp.zeros((), power_bins.dtype), lax.add, (1, 2 * HALF + 1), (1, 1), ((0, 0), (HALF, HALF)))
        valid_seg = alive * (seg_number < seg_counts).astype(jnp.float32)
        factor = valid_seg[:, None] / jnp.sqrt(window_sum / window_count + epsilon)
        white_re = real_part * factor
        white_im = imag_part * factor
        padded_re = jnp.concatenate([white_re, zero_rows], axis=0)
        padded_im = jnp.concatenate([white_im, zero_rows], axis=0)
        slots = []
        for slot in range(K):
            partner_re = lax.dynamic_slice_in_dim(padded_re, offsets[slot], C, 0)
            partner_im = lax.dynamic_slice_in_dim(padded_im, offsets[slot], C, 0)
            slots.append(jnp.concatenate([white_re * partner_re + white_im * partner_im, white_im * partner_re - white_re * partner_im], axis=1))
        return (stacked + jnp.stack(slots, axis=1), None)
    initial = jnp.zeros((C, K, 2 * F), jnp.float32)
    seg_numbers = jnp.arange(SEGS, dtype=jnp.int32)
    stacked, unused = lax.scan(segment, initial, (traces, seg_numbers))
    padded_counts = jnp.concatenate([seg_counts, jnp.zeros((BAND,), jnp.int32)])
    divisors = []
    for slot in range(K):
        partner_count = lax.dynamic_slice_in_dim(padded_counts, offsets[slot], C, 0)
        divisors.append(jnp.maximum(jnp.minimum(seg_counts, partner_count), 1).astype(jnp.float32))
    divisor = jnp.stack(divisors, axis=1)
    cross = stacked / divisor[:, :, None]
    delay = delay_table(0, F, L, LAGS, F)
    return jnp.einsum('ckf,fl->ckl', cross, delay, precision=lax.Precision.HIGHEST)
```

```python
import functools
import math

import jax
import jax.numpy as jnp
import ml_dtypes
import numpy as np
from jax import lax
from jax.experimental import pallas as pl
from jax.experimental.pallas import tpu as pltpu
from jax.sharding import PartitionSpec as P

HALF = 32
LAGS = 512
F = 2048
W = 128
EPS = 1e-06
MESH = pl.DeviceIdType.MESH
F32 = jnp.float32
BF16 = jnp.bfloat16


def bins_of(freq, group, parity):
    m = np.arange(W)
    if freq == 0:
        return 2 * W * group + 2 * m + parity
    return F - 1 - (2 * W * group + 2 * m + 1 - parity)


def fourier_blocks(length):
    quarter = length // 4
    t = np.arange(quarter)[:, None]
    wave = 2.0 * math.pi * np.arange(length) / length
    cos = np.cos(wave).astype(np.float32).astype(ml_dtypes.bfloat16)
    sin = (-np.sin(wave)).astype(np.float32).astype(ml_dtypes.bfloat16)
    groups = F // 2 // (2 * W)
    out = np.empty((2, groups // 2, 4, quarter, 2 * W), ml_dtypes.bfloat16)
    for freq in range(2):
        for h in range(groups // 2):
            for parity in range(2):
                bins = np.concatenate([bins_of(freq, 2 * h + i, parity) for i in range(2)])
                phase = t * bins[None, :] % length
                out[freq, h, 2 * parity] = cos[phase]
                out[freq, h, 2 * parity + 1] = sin[phase]
                if parity == 1:
                    out[freq, h, 3, 0] = sin[quarter * bins % length]
    return out


def delay_blocks(length, chunks):
    shifts = np.arange(LAGS)[None, :] - LAGS // 2
    out = np.empty((2, chunks, 2 * W, LAGS), ml_dtypes.bfloat16)
    for freq in range(2):
        sign = -1.0 if freq == 0 else 1.0
        for q in range(chunks):
            phase = bins_of(freq, q // 2, q % 2)[:, None] * shifts % length * (2.0 * math.pi / length)
            out[freq, q, :W] = (np.cos(phase) / math.sqrt(F)).astype(np.float32)
            out[freq, q, W:] = (sign * np.sin(phase) / math.sqrt(F)).astype(np.float32)
    return out


def dot(a, b):
    return jnp.dot(a, b, preferred_element_type=F32)


def iota(shape, dim):
    return lax.broadcasted_iota(jnp.int32, shape, dim)


def kernel(
    nz, ns, segs, chunks, slots, offs, traces, dead, cnt, four, delay, out,
    tr, crecv, inverse, table, dly, lhs, mid, band, spec, power, near, own, recv, sel, mask, total, hoth, hrecv, fsend, frecv, vsum, srecv,
    tr_sem, c_send, c_recv, tab_sem, dly_sem, p_send, p_recv, w_send, w_recv, h_send, h_recv, f_send, f_recv, s_send, s_recv,
):
    z = lax.axis_index("chan")
    s_me = lax.axis_index("seg")
    fq = lax.axis_index("freq")
    up = fq == 1
    groups = chunks // 2
    wide = 2 * W
    half_blocks = traces.shape[1] // 2 // wide
    rows = own.shape[1]
    per = W // ns
    step = 2 * fq - 1
    dst = z + step
    src = z - step
    has_dst = jnp.logical_and(dst >= 0, dst < nz)
    has_src = jnp.logical_and(src >= 0, src < nz)
    twin = 1 - fq

    def table_copy(h):
        return pltpu.make_async_copy(four.at[fq, h], table.at[h], tab_sem.at[h])

    def trace_copy(s):
        return pltpu.make_async_copy(
            traces.at[pl.ds(s * W, W)], tr.at[pl.ds(s * W, W)], tr_sem.at[s]
        )

    trace_copy(0).start()
    for h in range(groups // 2):
        table_copy(h).start()
    for s in range(1, segs):
        trace_copy(s).start()
    delay_copy = pltpu.make_async_copy(delay.at[fq], dly, dly_sem)
    delay_copy.start()

    sends_h = jnp.logical_and(up, z > 0)
    takes_h = z < nz - 1
    barrier = pltpu.get_barrier_semaphore()

    @pl.when(has_src)
    def _():
        pl.semaphore_signal(barrier, inc=1, device_id={"chan": src}, device_id_type=MESH)

    pl.semaphore_signal(barrier, inc=1, device_id={"freq": twin}, device_id_type=MESH)
    for d in range(1, ns):
        pl.semaphore_signal(
            barrier, inc=1, device_id={"seg": lax.rem(s_me + d, ns)}, device_id_type=MESH
        )

    @pl.when(takes_h)
    def _():
        for d in range(ns):
            giver = {"chan": z + 1, "seg": lax.rem(s_me + d, ns), "freq": 1}
            pl.semaphore_signal(barrier, inc=1, device_id=giver, device_id_type=MESH)

    diag = iota((W, W), 0) == iota((W, W), 1)
    cnt_col = jnp.sum(jnp.where(diag, cnt[...], 0).astype(F32), axis=1, keepdims=True)
    live_col = jnp.sum(jnp.where(diag, dead[...], 0).astype(F32), axis=1, keepdims=True)
    for s in range(segs):
        seg_number = (s_me * segs + s).astype(F32)
        valid = jnp.where(seg_number < cnt_col, live_col, 0.0)
        mask[s * W : (s + 1) * W, :] = jnp.broadcast_to(valid, (W, W))
    for k in range(slots):
        target = (iota((W, 2 * W), 0) - step * offs[k] + 2 * W) & (2 * W - 1)
        sel[k * W : (k + 1) * W, :] = jnp.where(iota((W, 2 * W), 1) == target, 1.0, 0.0).astype(BF16)

    @pl.when(jnp.logical_not(has_src))
    def _():
        def clear(q, carry):
            recv[q] = jnp.zeros((rows, 2 * W), BF16)
            return carry

        lax.fori_loop(0, chunks, clear, 0)
        crecv[...] = jnp.zeros_like(crecv)

    @pl.when(jnp.logical_not(takes_h))
    def _():
        hrecv[...] = jnp.zeros_like(hrecv)

    alternate = (1 - 2 * (iota((1, W), 1) & 1)).astype(F32) * (1 - 2 * fq).astype(F32)

    def place(lane, core):
        return 2 * (lane & (W - 1)) + ((lane >> 7) ^ core)

    row_lane = iota((wide, wide), 0)
    col = place(iota((wide, wide), 1), fq)
    inside = place(row_lane, fq)
    around = inside + jnp.where((row_lane & (W - 1)) < W // 2, wide, -wide)
    across = 2 * wide - 1 - place(row_lane, twin)
    for i, at in enumerate((inside, around, across)):
        band[i * wide : (i + 1) * wide, :] = jnp.where(jnp.abs(at - col) <= HALF, 1.0, 0.0).astype(BF16)
    flip = jnp.where(iota((wide, wide), 0) + iota((wide, wide), 1) == wide, 1.0, 0.0).astype(BF16)
    first_lane = iota((W, W), 1) == 0
    low_lane = (iota((1, wide), 1) & (W - 1)) < W // 2

    def at_first(new, old):
        return jnp.concatenate([jnp.where(first_lane, new[:, :W], old[:, :W]), old[:, W:]], axis=1)

    def fold(at):
        def x(j):
            return tr[at, j * wide : (j + 1) * wide]

        quads = half_blocks // 2
        back = dot(
            jnp.concatenate(
                [x(half_blocks - 1 - j) for j in range(quads)]
                + [x(2 * half_blocks - 1 - j) for j in range(quads)],
                axis=0,
            ),
            flip,
        )
        for j in range(quads):
            a = x(j).astype(F32)
            b = x(half_blocks + j).astype(F32)
            a_back = back[j * W : (j + 1) * W]
            b_back = back[(quads + j) * W : (quads + j + 1) * W]
            if j > 0:
                a_back = at_first(x(half_blocks - j).astype(F32), a_back)
                b_back = at_first(x(2 * half_blocks - j).astype(F32), b_back)
            even, odd = a + b, a - b
            even_back, odd_back = a_back + b_back, a_back - b_back
            odd_sin = odd + odd_back
            if j == 0:
                a_mid = x(quads).astype(F32)
                b_mid = x(half_blocks + quads).astype(F32)
                odd_sin = at_first(a_mid - b_mid, odd_sin)
                mid[...] = (a_mid + b_mid)[:, :1] * alternate
            for i, term in enumerate((even + even_back, even - even_back, odd - odd_back, odd_sin)):
                high = term.astype(BF16)
                lhs[i, :W, j * wide : (j + 1) * wide] = high
                lhs[i, W:, j * wide : (j + 1) * wide] = (term - high.astype(F32)).astype(BF16)

    def transform(h, at):
        def part(i):
            both = dot(lhs[i], table[h, i])
            return both[:W] + both[W:]

        middle = mid[...]
        for parity in range(2):
            re = part(2 * parity)
            im = part(2 * parity + 1)
            if parity == 0:
                re = re + jnp.concatenate([middle, middle], axis=1)
            square = (re * re + im * im).astype(BF16)
            for i in range(2):
                lanes = slice(i * W, (i + 1) * W)
                spec[4 * h + 2 * i + parity, at, :W] = re[:, lanes]
                spec[4 * h + 2 * i + parity, at, W:] = im[:, lanes]
                power[2 * h + i, at, parity * W : (parity + 1) * W] = square[:, lanes]

    def whiten(g, at, factors):
        around = jnp.where(
            low_lane,
            power[g + 1, at, :] if g + 1 < groups else jnp.zeros((), BF16),
            power[g - 1, at, :] if g > 0 else jnp.zeros((), BF16),
        )
        parts = [power[g, at, :], around]
        if g + 1 == groups:
            parts.append(near[at, :])
        window = dot(jnp.concatenate(parts, axis=1), band[: len(parts) * wide, :])
        u = g * wide + place(iota((1, wide), 1), fq)
        number = (jnp.minimum(u, HALF) + HALF + 1).astype(F32)
        factor = jnp.concatenate([factors, factors], axis=1) * lax.rsqrt(window / number + EPS)
        for parity in range(2):
            scale = factor[:, parity * W : (parity + 1) * W]
            q = 2 * g + parity
            own[q, at, :W] = (spec[q, at, :W] * scale).astype(BF16)
            own[q, at, W:] = (spec[q, at, W:] * scale).astype(BF16)

    def power_copy(s):
        return pltpu.make_async_remote_copy(
            src_ref=power.at[groups - 1, rows_of(s)], dst_ref=near.at[rows_of(s)],
            send_sem=p_send.at[s], recv_sem=p_recv.at[s],
            device_id={"freq": twin}, device_id_type=MESH,
        )

    def white_copy(q, at):
        return pltpu.make_async_remote_copy(
            src_ref=own.at[q, at], dst_ref=recv.at[q, at],
            send_sem=w_send.at[q], recv_sem=w_recv.at[q],
            device_id={"chan": dst}, device_id_type=MESH,
        )

    def send(q, at):
        @pl.when(has_dst)
        def _():
            white_copy(q, at).start()

    whole = pl.ds(0, rows)

    def rows_of(s):
        return pl.ds(pl.multiple_of(s * W, W), W)

    count_copy = pltpu.make_async_remote_copy(
        src_ref=cnt, dst_ref=crecv, send_sem=c_send, recv_sem=c_recv,
        device_id={"chan": dst}, device_id_type=MESH,
    )
    peers = ns + has_dst.astype(jnp.int32) + 2 * ns * sends_h.astype(jnp.int32)

    def segment(s, first):
        at = rows_of(s)
        trace_copy(s).wait()
        fold(at)
        if first:
            table_copy(0).wait()
        transform(0, at)
        whiten_rows = mask[at, :]
        whiten(0, at, whiten_rows)
        if first:
            pl.semaphore_wait(barrier, peers)

            @pl.when(has_dst)
            def _():
                count_copy.start()

        send(0, at)
        send(1, at)
        for h in range(1, groups // 2):
            if first:
                table_copy(h).wait()
            transform(h, at)
        power_copy(s).start()
        whiten(1, at, whiten_rows)
        send(2, at)
        send(3, at)

    segment(0, True)

    def later(s, carry):
        segment(s, False)
        return carry

    lax.fori_loop(1, segs, later, 0)

    def finish(g, s):
        at = rows_of(s)
        whiten(g, at, mask[at, :])

    for g in range(2, groups):
        def each(s, carry, g=g):
            if g + 1 == groups:
                power_copy(s).wait_recv()
            finish(g, s)
            return carry

        lax.fori_loop(0, segs, each, 0)
        send(2 * g, whole)
        send(2 * g + 1, whole)
    delay_copy.wait()
    total[...] = jnp.zeros_like(total)

    @pl.when(has_src)
    def _():
        count_copy.wait_recv()

    counts = jnp.concatenate([cnt[...], crecv[...]], axis=1)
    for k in range(slots):
        target = (iota((W, 2 * W), 0) - step * offs[k] + 2 * W) & (2 * W - 1)
        partner = jnp.where(iota((W, 2 * W), 1) == target, counts, 0).astype(F32)
        fewer = jnp.minimum(cnt_col, jnp.sum(partner, axis=1, keepdims=True))
        inverse[k] = jnp.broadcast_to(1.0 / jnp.maximum(fewer, 1.0), (W, W))

    def correlate(q, carry):
        @pl.when(has_src)
        def _():
            white_copy(q, whole).wait_recv()

        re = [None] * slots
        im = [None] * slots
        for s in range(segs):
            at = slice(s * W, (s + 1) * W)
            mine = own[q, at, :]
            pair = dot(sel[...], jnp.concatenate([mine, recv[q, at, :]], axis=0))
            my_re = mine[:, :W].astype(F32)
            my_im = mine[:, W:].astype(F32)
            for k in range(slots):
                pair_re = pair[k * W : (k + 1) * W, :W]
                pair_im = pair[k * W : (k + 1) * W, W:]
                one = my_re * pair_re + my_im * pair_im
                two = my_im * pair_re - my_re * pair_im
                re[k] = one if s == 0 else re[k] + one
                im[k] = two if s == 0 else im[k] + two
        for k in range(slots):
            scale = inverse[k]
            cross = jnp.concatenate([re[k] * scale, im[k] * scale], axis=1).astype(BF16)
            total[k] += dot(cross, dly[q])
        return carry

    lax.fori_loop(0, chunks, correlate, 0)

    gap = iota((W, W), 1) - iota((W, W), 0)
    half = LAGS // 2

    def h_copy(d, q):
        peer = lax.rem(s_me + d, ns)
        return pltpu.make_async_remote_copy(
            src_ref=hoth.at[:, pl.ds(pl.multiple_of(peer * per, per), per), q * half : (q + 1) * half],
            dst_ref=hrecv.at[d], send_sem=h_send.at[d, q], recv_sem=h_recv.at[d],
            device_id={"chan": z - 1, "seg": peer, "freq": q}, device_id_type=MESH,
        )

    f_copy = pltpu.make_async_remote_copy(
        src_ref=fsend, dst_ref=frecv, send_sem=f_send, recv_sem=f_recv,
        device_id={"freq": twin}, device_id_type=MESH,
    )

    def s_copy(d):
        peer = lax.rem(s_me + d, ns)
        return pltpu.make_async_remote_copy(
            src_ref=vsum.at[:, pl.ds(pl.multiple_of(peer * per, per), per)],
            dst_ref=srecv.at[d - 1], send_sem=s_send.at[d - 1], recv_sem=s_recv.at[d - 1],
            device_id={"seg": peer}, device_id_type=MESH,
        )

    @pl.when(up)
    def _():
        for k in range(slots):
            moved = dot(jnp.where(gap == offs[k] - W, 1.0, 0.0).astype(BF16), total[k].astype(BF16))
            hoth[k] = moved.astype(BF16)

        @pl.when(sends_h)
        def _():
            for d in reversed(range(ns)):
                for q in range(2):
                    h_copy(d, q).start()

        for k in range(slots):
            total[k] = dot(jnp.where(gap == offs[k], 1.0, 0.0).astype(BF16), total[k].astype(BF16))

    kept = pl.ds(pl.multiple_of(fq * half, half), half)
    given = pl.ds(pl.multiple_of(twin * half, half), half)
    for k in range(slots):
        fsend[k] = total[k, :, given].astype(BF16)
    f_copy.start()
    f_copy.wait_recv()
    for k in range(slots):
        merged = total[k, :, kept] + frecv[k].astype(F32)
        total[k, :, kept] = merged
        vsum[k] = merged.astype(BF16)
    for d in range(1, ns):
        s_copy(d).start()
    for d in range(1, ns):
        s_copy(d).wait_recv()

    @pl.when(takes_h)
    def _():
        for d in range(ns):
            h_copy(d, 0).wait_recv()

    for k in range(slots):
        result = total[k, pl.ds(pl.multiple_of(s_me * per, per), per), kept]
        for d in range(1, ns):
            result += srecv[d - 1, k].astype(F32)
        for d in range(ns):
            result += hrecv[d, k].astype(F32)
        out[k] = result

    @pl.when(has_dst)
    def _():
        def drain(q, carry):
            white_copy(q, whole).wait_send()
            return carry

        lax.fori_loop(0, chunks, drain, 0)
        count_copy.wait_send()

    @pl.when(sends_h)
    def _():
        for d in range(ns):
            for q in range(2):
                h_copy(d, q).wait_send()

    for s in range(segs):
        power_copy(s).wait_send()
    f_copy.wait_send()
    for d in range(1, ns):
        s_copy(d).wait_send()


def shards(traces, dead_mask, seg_counts, offsets):
    segs, chans, length = traces.shape
    nz, ns = lax.axis_size("chan"), lax.axis_size("seg")
    slots = offsets.shape[0]
    chunks = F // 2 // W
    rows = segs * chans
    per = chans // ns
    half = LAGS // 2
    vmem = pl.BlockSpec(memory_space=pltpu.VMEM)
    hbm = pl.BlockSpec(memory_space=pl.ANY)
    dma = pltpu.SemaphoreType.DMA
    terms = pl.pallas_call(
        functools.partial(kernel, nz, ns, segs, chunks, slots),
        out_shape=jax.ShapeDtypeStruct((slots, per, half), F32),
        in_specs=[pl.BlockSpec(memory_space=pltpu.SMEM), hbm, vmem, vmem, hbm, hbm],
        out_specs=vmem,
        scratch_shapes=[
            pltpu.VMEM((rows, length), BF16),
            pltpu.VMEM((1, chans), jnp.int32),
            pltpu.VMEM((slots, W, W), F32),
            pltpu.VMEM((chunks // 4, 4, length // 4, 2 * W), BF16),
            pltpu.VMEM((chunks, 2 * W, LAGS), BF16),
            pltpu.VMEM((4, 2 * W, length // 4), BF16),
            pltpu.VMEM((W, W), F32),
            pltpu.VMEM((6 * W, 2 * W), BF16),
            pltpu.VMEM((chunks, rows, 2 * W), F32),
            pltpu.VMEM((chunks // 2, rows, 2 * W), BF16),
            pltpu.VMEM((rows, 2 * W), BF16),
            pltpu.VMEM((chunks, rows, 2 * W), BF16),
            pltpu.VMEM((chunks, rows, 2 * W), BF16),
            pltpu.VMEM((slots * W, 2 * W), BF16),
            pltpu.VMEM((rows, W), F32),
            pltpu.VMEM((slots, W, LAGS), F32),
            pltpu.VMEM((slots, W, LAGS), BF16),
            pltpu.VMEM((ns, slots, per, half), BF16),
            pltpu.VMEM((slots, W, half), BF16),
            pltpu.VMEM((slots, W, half), BF16),
            pltpu.VMEM((slots, W, half), BF16),
            pltpu.VMEM((max(ns - 1, 1), slots, per, half), BF16),
            dma((segs,)),
            dma,
            dma,
            dma((chunks // 4,)),
            dma,
            dma((segs,)),
            dma((segs,)),
            dma((chunks,)),
            dma((chunks,)),
            dma((ns, 2)),
            dma((ns,)),
            dma,
            dma,
            dma((max(ns - 1, 1),)),
            dma((max(ns - 1, 1),)),
        ],
        compiler_params=pltpu.CompilerParams(
            collective_id=0, has_side_effects=True, vmem_limit_bytes=56 * 1024 * 1024
        ),
    )(
        offsets,
        traces.reshape(rows, length),
        dead_mask.reshape(1, chans),
        seg_counts.reshape(1, chans),
        jnp.asarray(fourier_blocks(length)),
        jnp.asarray(delay_blocks(length, chunks)),
    )
    return jnp.transpose(terms, (1, 0, 2))


def solution(mesh):
    in_specs = (
        P("seg", ("groups", "chan"), None),
        P(("groups", "chan")),
        P(("groups", "chan")),
        P(),
    )
    out_specs = P(("groups", "chan", "seg"), None, "freq")
    return jax.shard_map(shards, mesh=mesh, in_specs=in_specs, out_specs=out_specs, check_vma=False)
```

```python
import functools
import math

import jax
import jax.numpy as jnp
import ml_dtypes
import numpy as np
from jax import lax
from jax.experimental import pallas as pl
from jax.experimental.pallas import tpu as pltpu
from jax.sharding import PartitionSpec as P

HALF = 32
LAGS = 512
F = 2048
W = 128
EPS = 1e-06
MESH = pl.DeviceIdType.MESH
F32 = jnp.float32
BF16 = jnp.bfloat16


def bins_of(freq, group, parity):
    m = np.arange(W)
    if freq == 0:
        return 2 * W * group + 2 * m + parity
    return F - 1 - (2 * W * group + 2 * m + 1 - parity)


def fourier_blocks(length):
    quarter = length // 4
    t = np.arange(quarter)[:, None]
    wave = 2.0 * math.pi * np.arange(length) / length
    cos = np.cos(wave).astype(np.float32).astype(ml_dtypes.bfloat16)
    sin = (-np.sin(wave)).astype(np.float32).astype(ml_dtypes.bfloat16)
    groups = F // 2 // (2 * W)
    out = np.empty((2, groups // 2, 4, quarter, 2 * W), ml_dtypes.bfloat16)
    for freq in range(2):
        for h in range(groups // 2):
            for parity in range(2):
                bins = np.concatenate([bins_of(freq, 2 * h + i, parity) for i in range(2)])
                phase = t * bins[None, :] % length
                out[freq, h, 2 * parity] = cos[phase]
                out[freq, h, 2 * parity + 1] = sin[phase]
                if parity == 1:
                    out[freq, h, 3, 0] = sin[quarter * bins % length]
    return out


def delay_blocks(length, chunks):
    shifts = np.arange(LAGS)[None, :] - LAGS // 2
    out = np.empty((2, chunks, 2 * W, LAGS), ml_dtypes.bfloat16)
    for freq in range(2):
        sign = -1.0 if freq == 0 else 1.0
        for q in range(chunks):
            phase = bins_of(freq, q // 2, q % 2)[:, None] * shifts % length * (2.0 * math.pi / length)
            out[freq, q, :W] = (np.cos(phase) / math.sqrt(F)).astype(np.float32)
            out[freq, q, W:] = (sign * np.sin(phase) / math.sqrt(F)).astype(np.float32)
    return out


def dot(a, b):
    return jnp.dot(a, b, preferred_element_type=F32)


def iota(shape, dim):
    return lax.broadcasted_iota(jnp.int32, shape, dim)


def kernel(
    nz, ns, segs, chunks, slots, offs_in, traces, dead_in, cnt_in, four, delay, out,
    offs, dead, cnt,
    tr, crecv, inverse, table, dly, lhs, mid, band, spec, power, near, own, recv, sel, mask, total, hoth, hrecv, fsend, frecv, vsum, srecv,
    in_sem, tr_sem, c_send, c_recv, tab_sem, dly_sem, p_send, p_recv, w_send, w_recv, h_send, h_recv, f_send, f_recv, s_send, s_recv,
):
    z = lax.axis_index("chan")
    s_me = lax.axis_index("seg")
    fq = lax.axis_index("freq")
    up = fq == 1
    groups = chunks // 2
    wide = 2 * W
    half_blocks = traces.shape[1] // 2 // wide
    rows = own.shape[1]
    per = W // ns
    step = 2 * fq - 1
    dst = z + step
    src = z - step
    has_dst = jnp.logical_and(dst >= 0, dst < nz)
    has_src = jnp.logical_and(src >= 0, src < nz)
    twin = 1 - fq

    def table_copy(h):
        return pltpu.make_async_copy(four.at[fq, h], table.at[h], tab_sem.at[h])

    def trace_copy(s):
        return pltpu.make_async_copy(
            traces.at[pl.ds(s * W, W)], tr.at[pl.ds(s * W, W)], tr_sem.at[s]
        )

    small = [
        pltpu.make_async_copy(a, b, in_sem.at[i])
        for i, (a, b) in enumerate(((offs_in, offs), (dead_in, dead), (cnt_in, cnt)))
    ]
    for copy in small:
        copy.start()
    trace_copy(0).start()
    for h in range(groups // 2):
        table_copy(h).start()
    for s in range(1, segs):
        trace_copy(s).start()
    delay_copy = pltpu.make_async_copy(delay.at[fq], dly, dly_sem)
    delay_copy.start()

    sends_h = jnp.logical_and(up, z > 0)
    takes_h = z < nz - 1
    barrier = pltpu.get_barrier_semaphore()

    @pl.when(has_src)
    def _():
        pl.semaphore_signal(barrier, inc=1, device_id={"chan": src}, device_id_type=MESH)

    pl.semaphore_signal(barrier, inc=1, device_id={"freq": twin}, device_id_type=MESH)
    for d in range(1, ns):
        pl.semaphore_signal(
            barrier, inc=1, device_id={"seg": lax.rem(s_me + d, ns)}, device_id_type=MESH
        )

    @pl.when(takes_h)
    def _():
        for d in range(ns):
            giver = {"chan": z + 1, "seg": lax.rem(s_me + d, ns), "freq": 1}
            pl.semaphore_signal(barrier, inc=1, device_id=giver, device_id_type=MESH)

    for copy in small:
        copy.wait()
    diag = iota((W, W), 0) == iota((W, W), 1)
    cnt_col = jnp.sum(jnp.where(diag, cnt[...], 0).astype(F32), axis=1, keepdims=True)
    live_col = jnp.sum(jnp.where(diag, dead[...], 0).astype(F32), axis=1, keepdims=True)
    for s in range(segs):
        seg_number = (s_me * segs + s).astype(F32)
        valid = jnp.where(seg_number < cnt_col, live_col, 0.0)
        mask[s * W : (s + 1) * W, :] = jnp.broadcast_to(valid, (W, W))
    for k in range(slots):
        target = (iota((W, 2 * W), 0) - step * offs[k] + 2 * W) & (2 * W - 1)
        sel[k * W : (k + 1) * W, :] = jnp.where(iota((W, 2 * W), 1) == target, 1.0, 0.0).astype(BF16)

    @pl.when(jnp.logical_not(has_src))
    def _():
        def clear(q, carry):
            recv[q] = jnp.zeros((rows, 2 * W), BF16)
            return carry

        lax.fori_loop(0, chunks, clear, 0)
        crecv[...] = jnp.zeros_like(crecv)

    @pl.when(jnp.logical_not(takes_h))
    def _():
        hrecv[...] = jnp.zeros_like(hrecv)

    alternate = (1 - 2 * (iota((1, W), 1) & 1)).astype(F32) * (1 - 2 * fq).astype(F32)

    def place(lane, core):
        return 2 * (lane & (W - 1)) + ((lane >> 7) ^ core)

    row_lane = iota((wide, wide), 0)
    col = place(iota((wide, wide), 1), fq)
    inside = place(row_lane, fq)
    around = inside + jnp.where((row_lane & (W - 1)) < W // 2, wide, -wide)
    across = 2 * wide - 1 - place(row_lane, twin)
    for i, at in enumerate((inside, around, across)):
        band[i * wide : (i + 1) * wide, :] = jnp.where(jnp.abs(at - col) <= HALF, 1.0, 0.0).astype(BF16)
    flip = jnp.where(iota((wide, wide), 0) + iota((wide, wide), 1) == wide, 1.0, 0.0).astype(BF16)
    first_lane = iota((W, W), 1) == 0
    low_lane = (iota((1, wide), 1) & (W - 1)) < W // 2

    def at_first(new, old):
        return jnp.concatenate([jnp.where(first_lane, new[:, :W], old[:, :W]), old[:, W:]], axis=1)

    def fold(at):
        def x(j):
            return tr[at, j * wide : (j + 1) * wide]

        quads = half_blocks // 2
        back = dot(
            jnp.concatenate(
                [x(half_blocks - 1 - j) for j in range(quads)]
                + [x(2 * half_blocks - 1 - j) for j in range(quads)],
                axis=0,
            ),
            flip,
        )
        for j in range(quads):
            a = x(j).astype(F32)
            b = x(half_blocks + j).astype(F32)
            a_back = back[j * W : (j + 1) * W]
            b_back = back[(quads + j) * W : (quads + j + 1) * W]
            if j > 0:
                a_back = at_first(x(half_blocks - j).astype(F32), a_back)
                b_back = at_first(x(2 * half_blocks - j).astype(F32), b_back)
            even, odd = a + b, a - b
            even_back, odd_back = a_back + b_back, a_back - b_back
            odd_sin = odd + odd_back
            if j == 0:
                a_mid = x(quads).astype(F32)
                b_mid = x(half_blocks + quads).astype(F32)
                odd_sin = at_first(a_mid - b_mid, odd_sin)
                mid[...] = (a_mid + b_mid)[:, :1] * alternate
            for i, term in enumerate((even + even_back, even - even_back, odd - odd_back, odd_sin)):
                high = term.astype(BF16)
                lhs[i, :W, j * wide : (j + 1) * wide] = high
                lhs[i, W:, j * wide : (j + 1) * wide] = (term - high.astype(F32)).astype(BF16)

    def transform(h, at):
        def part(i):
            both = dot(lhs[i], table[h, i])
            return both[:W] + both[W:]

        middle = mid[...]
        for parity in range(2):
            re = part(2 * parity)
            im = part(2 * parity + 1)
            if parity == 0:
                re = re + jnp.concatenate([middle, middle], axis=1)
            square = (re * re + im * im).astype(BF16)
            for i in range(2):
                lanes = slice(i * W, (i + 1) * W)
                spec[4 * h + 2 * i + parity, at, :W] = re[:, lanes]
                spec[4 * h + 2 * i + parity, at, W:] = im[:, lanes]
                power[2 * h + i, at, parity * W : (parity + 1) * W] = square[:, lanes]

    def whiten(g, at, factors):
        around = jnp.where(
            low_lane,
            power[g + 1, at, :] if g + 1 < groups else jnp.zeros((), BF16),
            power[g - 1, at, :] if g > 0 else jnp.zeros((), BF16),
        )
        parts = [power[g, at, :], around]
        if g + 1 == groups:
            parts.append(near[at, :])
        window = dot(jnp.concatenate(parts, axis=1), band[: len(parts) * wide, :])
        u = g * wide + place(iota((1, wide), 1), fq)
        number = (jnp.minimum(u, HALF) + HALF + 1).astype(F32)
        factor = jnp.concatenate([factors, factors], axis=1) * lax.rsqrt(window / number + EPS)
        for parity in range(2):
            scale = factor[:, parity * W : (parity + 1) * W]
            q = 2 * g + parity
            own[q, at, :W] = (spec[q, at, :W] * scale).astype(BF16)
            own[q, at, W:] = (spec[q, at, W:] * scale).astype(BF16)

    def power_copy(s):
        return pltpu.make_async_remote_copy(
            src_ref=power.at[groups - 1, rows_of(s)], dst_ref=near.at[rows_of(s)],
            send_sem=p_send.at[s], recv_sem=p_recv.at[s],
            device_id={"freq": twin}, device_id_type=MESH,
        )

    def white_copy(q, at):
        return pltpu.make_async_remote_copy(
            src_ref=own.at[q, at], dst_ref=recv.at[q, at],
            send_sem=w_send.at[q], recv_sem=w_recv.at[q],
            device_id={"chan": dst}, device_id_type=MESH,
        )

    def send(q, at):
        @pl.when(has_dst)
        def _():
            white_copy(q, at).start()

    whole = pl.ds(0, rows)

    def rows_of(s):
        return pl.ds(pl.multiple_of(s * W, W), W)

    count_copy = pltpu.make_async_remote_copy(
        src_ref=cnt, dst_ref=crecv, send_sem=c_send, recv_sem=c_recv,
        device_id={"chan": dst}, device_id_type=MESH,
    )
    peers = ns + has_dst.astype(jnp.int32) + 2 * ns * sends_h.astype(jnp.int32)

    def segment(s, first):
        at = rows_of(s)
        trace_copy(s).wait()
        fold(at)
        if first:
            table_copy(0).wait()
        transform(0, at)
        whiten_rows = mask[at, :]
        whiten(0, at, whiten_rows)
        if first:
            pl.semaphore_wait(barrier, peers)

            @pl.when(has_dst)
            def _():
                count_copy.start()

        send(0, at)
        send(1, at)
        for h in range(1, groups // 2):
            if first:
                table_copy(h).wait()
            transform(h, at)
        power_copy(s).start()
        whiten(1, at, whiten_rows)
        send(2, at)
        send(3, at)

    segment(0, True)

    def later(s, carry):
        segment(s, False)
        return carry

    lax.fori_loop(1, segs, later, 0)

    def finish(g, s):
        at = rows_of(s)
        whiten(g, at, mask[at, :])

    for g in range(2, groups):
        def each(s, carry, g=g):
            if g + 1 == groups:
                power_copy(s).wait_recv()
            finish(g, s)
            return carry

        lax.fori_loop(0, segs, each, 0)
        send(2 * g, whole)
        send(2 * g + 1, whole)
    delay_copy.wait()
    total[...] = jnp.zeros_like(total)

    @pl.when(has_src)
    def _():
        count_copy.wait_recv()

    counts = jnp.concatenate([cnt[...], crecv[...]], axis=1)
    for k in range(slots):
        target = (iota((W, 2 * W), 0) - step * offs[k] + 2 * W) & (2 * W - 1)
        partner = jnp.where(iota((W, 2 * W), 1) == target, counts, 0).astype(F32)
        fewer = jnp.minimum(cnt_col, jnp.sum(partner, axis=1, keepdims=True))
        inverse[k] = jnp.broadcast_to(1.0 / jnp.maximum(fewer, 1.0), (W, W))

    def correlate(q, carry):
        @pl.when(has_src)
        def _():
            white_copy(q, whole).wait_recv()

        re = [None] * slots
        im = [None] * slots
        for s in range(segs):
            at = slice(s * W, (s + 1) * W)
            mine = own[q, at, :]
            pair = dot(sel[...], jnp.concatenate([mine, recv[q, at, :]], axis=0))
            my_re = mine[:, :W].astype(F32)
            my_im = mine[:, W:].astype(F32)
            for k in range(slots):
                pair_re = pair[k * W : (k + 1) * W, :W]
                pair_im = pair[k * W : (k + 1) * W, W:]
                one = my_re * pair_re + my_im * pair_im
                two = my_im * pair_re - my_re * pair_im
                re[k] = one if s == 0 else re[k] + one
                im[k] = two if s == 0 else im[k] + two
        for k in range(slots):
            scale = inverse[k]
            cross = jnp.concatenate([re[k] * scale, im[k] * scale], axis=1).astype(BF16)
            total[k] += dot(cross, dly[q])
        return carry

    lax.fori_loop(0, chunks, correlate, 0)

    gap = iota((W, W), 1) - iota((W, W), 0)
    half = LAGS // 2

    def h_copy(d, q):
        peer = lax.rem(s_me + d, ns)
        return pltpu.make_async_remote_copy(
            src_ref=hoth.at[:, pl.ds(pl.multiple_of(peer * per, per), per), q * half : (q + 1) * half],
            dst_ref=hrecv.at[d], send_sem=h_send.at[d, q], recv_sem=h_recv.at[d],
            device_id={"chan": z - 1, "seg": peer, "freq": q}, device_id_type=MESH,
        )

    f_copy = pltpu.make_async_remote_copy(
        src_ref=fsend, dst_ref=frecv, send_sem=f_send, recv_sem=f_recv,
        device_id={"freq": twin}, device_id_type=MESH,
    )

    def s_copy(d):
        peer = lax.rem(s_me + d, ns)
        return pltpu.make_async_remote_copy(
            src_ref=vsum.at[:, pl.ds(pl.multiple_of(peer * per, per), per)],
            dst_ref=srecv.at[d - 1], send_sem=s_send.at[d - 1], recv_sem=s_recv.at[d - 1],
            device_id={"seg": peer}, device_id_type=MESH,
        )

    @pl.when(up)
    def _():
        for k in range(slots):
            moved = dot(jnp.where(gap == offs[k] - W, 1.0, 0.0).astype(BF16), total[k].astype(BF16))
            hoth[k] = moved.astype(BF16)

        @pl.when(sends_h)
        def _():
            for d in reversed(range(ns)):
                for q in range(2):
                    h_copy(d, q).start()

        for k in range(slots):
            total[k] = dot(jnp.where(gap == offs[k], 1.0, 0.0).astype(BF16), total[k].astype(BF16))

    kept = pl.ds(pl.multiple_of(fq * half, half), half)
    given = pl.ds(pl.multiple_of(twin * half, half), half)
    for k in range(slots):
        fsend[k] = total[k, :, given].astype(BF16)
    f_copy.start()
    f_copy.wait_recv()
    for k in range(slots):
        merged = total[k, :, kept] + frecv[k].astype(F32)
        total[k, :, kept] = merged
        vsum[k] = merged.astype(BF16)
    for d in range(1, ns):
        s_copy(d).start()
    for d in range(1, ns):
        s_copy(d).wait_recv()

    @pl.when(takes_h)
    def _():
        for d in range(ns):
            h_copy(d, 0).wait_recv()

    for k in range(slots):
        result = total[k, pl.ds(pl.multiple_of(s_me * per, per), per), kept]
        for d in range(1, ns):
            result += srecv[d - 1, k].astype(F32)
        for d in range(ns):
            result += hrecv[d, k].astype(F32)
        out[:, k, :] = result

    @pl.when(has_dst)
    def _():
        def drain(q, carry):
            white_copy(q, whole).wait_send()
            return carry

        lax.fori_loop(0, chunks, drain, 0)
        count_copy.wait_send()

    @pl.when(sends_h)
    def _():
        for d in range(ns):
            for q in range(2):
                h_copy(d, q).wait_send()

    for s in range(segs):
        power_copy(s).wait_send()
    f_copy.wait_send()
    for d in range(1, ns):
        s_copy(d).wait_send()


def pin(x):
    return pltpu.with_memory_space_constraint(x, pltpu.HBM)


def shards(traces, dead_mask, seg_counts, offsets):
    segs, chans, length = traces.shape
    nz, ns = lax.axis_size("chan"), lax.axis_size("seg")
    slots = offsets.shape[0]
    chunks = F // 2 // W
    rows = segs * chans
    per = chans // ns
    half = LAGS // 2
    vmem = pl.BlockSpec(memory_space=pltpu.VMEM)
    hbm = pl.BlockSpec(memory_space=pltpu.HBM)
    dma = pltpu.SemaphoreType.DMA
    terms = pl.pallas_call(
        functools.partial(kernel, nz, ns, segs, chunks, slots),
        out_shape=jax.ShapeDtypeStruct((per, slots, half), F32),
        in_specs=[hbm] * 6,
        out_specs=vmem,
        scratch_shapes=[
            pltpu.SMEM((slots,), jnp.int32),
            pltpu.VMEM((1, chans), jnp.int32),
            pltpu.VMEM((1, chans), jnp.int32),
            pltpu.VMEM((rows, length), BF16),
            pltpu.VMEM((1, chans), jnp.int32),
            pltpu.VMEM((slots, W, W), F32),
            pltpu.VMEM((chunks // 4, 4, length // 4, 2 * W), BF16),
            pltpu.VMEM((chunks, 2 * W, LAGS), BF16),
            pltpu.VMEM((4, 2 * W, length // 4), BF16),
            pltpu.VMEM((W, W), F32),
            pltpu.VMEM((6 * W, 2 * W), BF16),
            pltpu.VMEM((chunks, rows, 2 * W), F32),
            pltpu.VMEM((chunks // 2, rows, 2 * W), BF16),
            pltpu.VMEM((rows, 2 * W), BF16),
            pltpu.VMEM((chunks, rows, 2 * W), BF16),
            pltpu.VMEM((chunks, rows, 2 * W), BF16),
            pltpu.VMEM((slots * W, 2 * W), BF16),
            pltpu.VMEM((rows, W), F32),
            pltpu.VMEM((slots, W, LAGS), F32),
            pltpu.VMEM((slots, W, LAGS), BF16),
            pltpu.VMEM((ns, slots, per, half), BF16),
            pltpu.VMEM((slots, W, half), BF16),
            pltpu.VMEM((slots, W, half), BF16),
            pltpu.VMEM((slots, W, half), BF16),
            pltpu.VMEM((max(ns - 1, 1), slots, per, half), BF16),
            dma((3,)),
            dma((segs,)),
            dma,
            dma,
            dma((chunks // 4,)),
            dma,
            dma((segs,)),
            dma((segs,)),
            dma((chunks,)),
            dma((chunks,)),
            dma((ns, 2)),
            dma((ns,)),
            dma,
            dma,
            dma((max(ns - 1, 1),)),
            dma((max(ns - 1, 1),)),
        ],
        compiler_params=pltpu.CompilerParams(
            collective_id=0, has_side_effects=True, vmem_limit_bytes=50 * 1024 * 1024
        ),
    )(
        pin(offsets),
        traces.reshape(rows, length),
        pin(dead_mask.reshape(1, chans)),
        pin(seg_counts.reshape(1, chans)),
        jnp.asarray(fourier_blocks(length)),
        jnp.asarray(delay_blocks(length, chunks)),
    )
    return terms


def solution(mesh):
    in_specs = (
        P("seg", ("groups", "chan"), None),
        P(("groups", "chan")),
        P(("groups", "chan")),
        P(),
    )
    out_specs = P(("groups", "chan", "seg"), None, "freq")
    return jax.shard_map(shards, mesh=mesh, in_specs=in_specs, out_specs=out_specs, check_vma=False)
```

```python
import functools
import math

import jax
import jax.numpy as jnp
import ml_dtypes
import numpy as np
from jax import lax
from jax.experimental import pallas as pl
from jax.experimental.pallas import tpu as pltpu
from jax.sharding import PartitionSpec as P

HALF = 32
LAGS = 512
F = 2048
W = 128
EPS = 1e-06
BLOCKS = 4
R = W // BLOCKS
DIRECT = (2, 3)
MESH = pl.DeviceIdType.MESH
F32 = jnp.float32
BF16 = jnp.bfloat16


def bins_of(freq, group, parity):
    m = np.arange(W)
    if freq == 0:
        return 2 * W * group + 2 * m + parity
    return F - 1 - (2 * W * group + 2 * m + 1 - parity)


def fourier_blocks(length):
    quarter = length // 4
    t = np.arange(quarter)[:, None]
    wave = 2.0 * math.pi * np.arange(length) / length
    cos = np.cos(wave).astype(np.float32).astype(ml_dtypes.bfloat16)
    sin = (-np.sin(wave)).astype(np.float32).astype(ml_dtypes.bfloat16)
    groups = F // 2 // (2 * W)
    out = np.empty((2, groups // 2, 4, quarter, 2 * W), ml_dtypes.bfloat16)
    for freq in range(2):
        for h in range(groups // 2):
            for parity in range(2):
                bins = np.concatenate([bins_of(freq, 2 * h + i, parity) for i in range(2)])
                phase = t * bins[None, :] % length
                out[freq, h, 2 * parity] = cos[phase]
                out[freq, h, 2 * parity + 1] = sin[phase]
                if parity == 1:
                    out[freq, h, 3, 0] = sin[quarter * bins % length]
    return out


def delay_blocks(length, chunks):
    shifts = np.arange(LAGS)[None, :] - LAGS // 2
    out = np.empty((2, chunks, 2 * W, LAGS), ml_dtypes.bfloat16)
    for freq in range(2):
        for q in range(chunks):
            phase = bins_of(freq, q // 2, q % 2)[:, None] * shifts % length * (2.0 * math.pi / length)
            out[freq, q, :W] = (np.cos(phase) / math.sqrt(F)).astype(np.float32)
            out[freq, q, W:] = (-np.sin(phase) / math.sqrt(F)).astype(np.float32)
    return out


def dot(a, b):
    return jnp.dot(a, b, preferred_element_type=F32)


def iota(shape, dim):
    return lax.broadcasted_iota(jnp.int32, shape, dim)


def kernel(
    nz, ns, segs, chunks, slots, offs_in, traces, dead_in, cnt_in, four, delay, out,
    offs, dead, cnt,
    tr, crecv, inverse, table, dly, lhs, mid, band, spec, power, near, own, recv, own_last, recv_last, sel, mask, total,
    hbuf, hxr, hz, hred, hdir, fsend, frecv, vsum, srecv,
    in_sem, tr_sem, c_send, c_recv, tab_sem, dly_sem, p_send, p_recv, w_send, w_recv, t_send, t_recv, hx_send, hx_recv, hz_send, hz_recv,
    hd_send, hd_recv, f_send, f_recv, s_send, s_recv,
):
    z = lax.axis_index("chan")
    s_me = lax.axis_index("seg")
    fq = lax.axis_index("freq")
    up = fq == 1
    groups = chunks // 2
    wide = 2 * W
    half_blocks = traces.shape[1] // 2 // wide
    rows = own.shape[1]
    per = W // ns
    step = 2 * fq - 1
    dst = z + step
    src = z - step
    has_dst = jnp.logical_and(dst >= 0, dst < nz)
    has_src = jnp.logical_and(src >= 0, src < nz)
    twin = 1 - fq

    def table_copy(h):
        return pltpu.make_async_copy(four.at[fq, h], table.at[h], tab_sem.at[h])

    def trace_copy(s):
        return pltpu.make_async_copy(
            traces.at[pl.ds(s * W, W)], tr.at[pl.ds(s * W, W)], tr_sem.at[s]
        )

    small = [
        pltpu.make_async_copy(a, b, in_sem.at[i])
        for i, (a, b) in enumerate(((offs_in, offs), (dead_in, dead), (cnt_in, cnt)))
    ]
    for copy in small:
        copy.start()
    trace_copy(0).start()
    for h in range(groups // 2):
        table_copy(h).start()
    for s in range(1, segs):
        trace_copy(s).start()
    delay_copy = pltpu.make_async_copy(delay.at[fq], dly, dly_sem)
    delay_copy.start()

    sends_h = jnp.logical_and(up, z > 0)
    takes_h = z < nz - 1
    barrier = pltpu.get_barrier_semaphore()

    @pl.when(has_src)
    def _():
        pl.semaphore_signal(barrier, inc=1, device_id={"chan": src}, device_id_type=MESH)

    pl.semaphore_signal(barrier, inc=1, device_id={"freq": twin}, device_id_type=MESH)
    for d in range(1, ns):
        pl.semaphore_signal(
            barrier, inc=1, device_id={"seg": lax.rem(s_me + d, ns)}, device_id_type=MESH
        )

    @pl.when(takes_h)
    def _():
        for d in range(ns):
            giver = {"chan": z + 1, "seg": lax.rem(s_me + d, ns), "freq": 1}
            pl.semaphore_signal(barrier, inc=1, device_id=giver, device_id_type=MESH)

    for copy in small:
        copy.wait()
    diag = iota((W, W), 0) == iota((W, W), 1)
    cnt_col = jnp.sum(jnp.where(diag, cnt[...], 0).astype(F32), axis=1, keepdims=True)
    live_col = jnp.sum(jnp.where(diag, dead[...], 0).astype(F32), axis=1, keepdims=True)
    for s in range(segs):
        seg_number = (s_me * segs + s).astype(F32)
        valid = jnp.where(seg_number < cnt_col, live_col, 0.0)
        mask[s * W : (s + 1) * W, :] = jnp.broadcast_to(valid, (W, W))
    turn = 2 * W - 1 - W * fq
    for k in range(slots):
        target = (iota((W, 2 * W), 0) + offs[k]) & turn
        sel[k * W : (k + 1) * W, :] = jnp.where(iota((W, 2 * W), 1) == target, 1.0, 0.0).astype(BF16)

    @pl.when(jnp.logical_not(takes_h))
    def _():
        hred[...] = jnp.zeros_like(hred)
        hdir[...] = jnp.zeros_like(hdir)
        crecv[...] = jnp.zeros_like(crecv)

    alternate = (1 - 2 * (iota((1, W), 1) & 1)).astype(F32) * (1 - 2 * fq).astype(F32)

    def place(lane, core):
        return 2 * (lane & (W - 1)) + ((lane >> 7) ^ core)

    row_lane = iota((wide, wide), 0)
    col = place(iota((wide, wide), 1), fq)
    inside = place(row_lane, fq)
    around = inside + jnp.where((row_lane & (W - 1)) < W // 2, wide, -wide)
    across = 2 * wide - 1 - place(row_lane, twin)
    for i, at in enumerate((inside, around, across)):
        band[i * wide : (i + 1) * wide, :] = jnp.where(jnp.abs(at - col) <= HALF, 1.0, 0.0).astype(BF16)
    flip = jnp.where(iota((wide, wide), 0) + iota((wide, wide), 1) == wide, 1.0, 0.0).astype(BF16)
    first_lane = iota((W, W), 1) == 0
    low_lane = (iota((1, wide), 1) & (W - 1)) < W // 2

    def at_first(new, old):
        return jnp.concatenate([jnp.where(first_lane, new[:, :W], old[:, :W]), old[:, W:]], axis=1)

    def fold(at):
        def x(j):
            return tr[at, j * wide : (j + 1) * wide]

        quads = half_blocks // 2
        back = dot(
            jnp.concatenate(
                [x(half_blocks - 1 - j) for j in range(quads)]
                + [x(2 * half_blocks - 1 - j) for j in range(quads)],
                axis=0,
            ),
            flip,
        )
        for j in range(quads):
            a = x(j).astype(F32)
            b = x(half_blocks + j).astype(F32)
            a_back = back[j * W : (j + 1) * W]
            b_back = back[(quads + j) * W : (quads + j + 1) * W]
            if j > 0:
                a_back = at_first(x(half_blocks - j).astype(F32), a_back)
                b_back = at_first(x(2 * half_blocks - j).astype(F32), b_back)
            even, odd = a + b, a - b
            even_back, odd_back = a_back + b_back, a_back - b_back
            odd_sin = odd + odd_back
            if j == 0:
                a_mid = x(quads).astype(F32)
                b_mid = x(half_blocks + quads).astype(F32)
                odd_sin = at_first(a_mid - b_mid, odd_sin)
                mid[...] = (a_mid + b_mid)[:, :1] * alternate
            for i, term in enumerate((even + even_back, even - even_back, odd - odd_back, odd_sin)):
                high = term.astype(BF16)
                lhs[i, :W, j * wide : (j + 1) * wide] = high
                lhs[i, W:, j * wide : (j + 1) * wide] = (term - high.astype(F32)).astype(BF16)

    def transform(h, at):
        def part(i):
            both = dot(lhs[i], table[h, i])
            return both[:W] + both[W:]

        middle = mid[...]
        for parity in range(2):
            re = part(2 * parity)
            im = part(2 * parity + 1)
            if parity == 0:
                re = re + jnp.concatenate([middle, middle], axis=1)
            square = (re * re + im * im).astype(BF16)
            for i in range(2):
                lanes = slice(i * W, (i + 1) * W)
                spec[4 * h + 2 * i + parity, at, :W] = re[:, lanes]
                spec[4 * h + 2 * i + parity, at, W:] = im[:, lanes]
                power[2 * h + i, at, parity * W : (parity + 1) * W] = square[:, lanes]

    def whiten(g, s, factors):
        at = rows_of(s)
        around = jnp.where(
            low_lane,
            power[g + 1, at, :] if g + 1 < groups else jnp.zeros((), BF16),
            power[g - 1, at, :] if g > 0 else jnp.zeros((), BF16),
        )
        parts = [power[g, at, :], around]
        if g + 1 == groups:
            parts.append(near[at, :])
        window = dot(jnp.concatenate(parts, axis=1), band[: len(parts) * wide, :])
        u = g * wide + place(iota((1, wide), 1), fq)
        number = (jnp.minimum(u, HALF) + HALF + 1).astype(F32)
        factor = jnp.concatenate([factors, factors], axis=1) * lax.rsqrt(window / number + EPS)
        for parity in range(2):
            scale = factor[:, parity * W : (parity + 1) * W]
            q = 2 * g + parity
            re = (spec[q, at, :W] * scale).astype(BF16)
            im = (spec[q, at, W:] * scale).astype(BF16)
            if q + 1 < chunks:
                own[q, at, :W] = re
                own[q, at, W:] = im
            else:
                for i in range(BLOCKS):
                    to = pl.ds(pl.multiple_of(s * R, R), R)
                    own_last[i, to, :W] = re[i * R : (i + 1) * R]
                    own_last[i, to, W:] = im[i * R : (i + 1) * R]

    def power_copy(s):
        return pltpu.make_async_remote_copy(
            src_ref=power.at[groups - 1, rows_of(s)], dst_ref=near.at[rows_of(s)],
            send_sem=p_send.at[s], recv_sem=p_recv.at[s],
            device_id={"freq": twin}, device_id_type=MESH,
        )

    def white_copy(q, at):
        return pltpu.make_async_remote_copy(
            src_ref=own.at[q, at], dst_ref=recv.at[q, at],
            send_sem=w_send.at[q], recv_sem=w_recv.at[q],
            device_id={"chan": dst}, device_id_type=MESH,
        )

    def last_copy(i):
        return pltpu.make_async_remote_copy(
            src_ref=own_last.at[i], dst_ref=recv_last.at[i],
            send_sem=t_send.at[i], recv_sem=t_recv.at[i],
            device_id={"chan": dst}, device_id_type=MESH,
        )

    def send(q, at):
        @pl.when(has_dst)
        def _():
            white_copy(q, at).start()

    whole = pl.ds(0, rows)

    def rows_of(s):
        return pl.ds(pl.multiple_of(s * W, W), W)

    count_copy = pltpu.make_async_remote_copy(
        src_ref=cnt, dst_ref=crecv, send_sem=c_send, recv_sem=c_recv,
        device_id={"chan": z - 1}, device_id_type=MESH,
    )
    peers = ns + has_dst.astype(jnp.int32) + 2 * ns * sends_h.astype(jnp.int32)

    def segment(s, first):
        at = rows_of(s)
        trace_copy(s).wait()
        fold(at)
        if first:
            table_copy(0).wait()
        transform(0, at)
        whiten_rows = mask[at, :]
        whiten(0, s, whiten_rows)
        if first:
            pl.semaphore_wait(barrier, peers)

            @pl.when(z > 0)
            def _():
                count_copy.start()

        send(0, at)
        send(1, at)
        for h in range(1, groups // 2):
            if first:
                table_copy(h).wait()
            transform(h, at)
        power_copy(s).start()
        whiten(1, s, whiten_rows)
        send(2, at)
        send(3, at)

    segment(0, True)

    def later(s, carry):
        segment(s, False)
        return carry

    lax.fori_loop(1, segs, later, 0)

    def finish(g, s):
        whiten(g, s, mask[rows_of(s), :])

    for g in range(2, groups):
        def each(s, carry, g=g):
            if g + 1 == groups:
                power_copy(s).wait_recv()
            finish(g, s)
            return carry

        lax.fori_loop(0, segs, each, 0)
        send(2 * g, whole)
        if g + 1 < groups:
            send(2 * g + 1, whole)

    @pl.when(has_dst)
    def _():
        for i in range(BLOCKS):
            last_copy(i).start()

    @pl.when(jnp.logical_not(has_src))
    def _():
        def clear(q, carry):
            recv[q] = jnp.zeros((rows, 2 * W), BF16)
            return carry

        lax.fori_loop(0, chunks - 1, clear, 0)
        recv_last[...] = jnp.zeros_like(recv_last)

    delay_copy.wait()
    total[...] = jnp.zeros_like(total)

    @pl.when(takes_h)
    def _():
        count_copy.wait_recv()

    counts = jnp.concatenate([cnt[...], crecv[...]], axis=1)
    for k in range(slots):
        partner = jnp.where(iota((W, 2 * W), 1) == iota((W, 2 * W), 0) + offs[k], counts, 0).astype(F32)
        fewer = jnp.minimum(cnt_col, jnp.sum(partner, axis=1, keepdims=True))
        inverse[k] = jnp.broadcast_to(1.0 / jnp.maximum(fewer, 1.0), (W, W))

    def below(k, first, number, width):
        return jnp.logical_and(iota((number, width), 0) + (offs[k] + first) >= W, up)

    def products(pieces, chosen, first, number):
        re = [None] * slots
        im = [None] * slots
        for s in range(segs):
            mine, theirs, both = pieces(s)
            pair = dot(chosen, both)
            mine = mine.astype(F32)
            theirs = theirs.astype(F32)
            for k in range(slots):
                other = below(k, first, number, W)
                my_re = jnp.where(other, theirs[:, :W], mine[:, :W])
                my_im = jnp.where(other, theirs[:, W:], mine[:, W:])
                pair_re = pair[k * number : (k + 1) * number, :W]
                pair_im = pair[k * number : (k + 1) * number, W:]
                one = my_re * pair_re + my_im * pair_im
                two = my_im * pair_re - my_re * pair_im
                re[k] = one if s == 0 else re[k] + one
                im[k] = two if s == 0 else im[k] + two
        return [jnp.concatenate([a, b], axis=1).astype(BF16) for a, b in zip(re, im)]

    def correlate(q, carry):
        @pl.when(has_src)
        def _():
            white_copy(q, whole).wait_recv()

        def pieces(s):
            at = slice(s * W, (s + 1) * W)
            mine, theirs = own[q, at, :], recv[q, at, :]
            return mine, theirs, jnp.concatenate([mine, theirs], axis=0)

        for k, cross in enumerate(products(pieces, sel[...], 0, W)):
            total[k] += dot(cross, dly[q])
        return carry

    half = LAGS // 2
    kept = pl.ds(pl.multiple_of(fq * half, half), half)
    given = pl.ds(pl.multiple_of(twin * half, half), half)
    held = BLOCKS // ns
    share = LAGS // ns
    mates = ns // 2

    def hx_copy(i, d):
        peer = lax.rem(s_me + d, ns)
        return pltpu.make_async_remote_copy(
            src_ref=hbuf.at[i, :, :, pl.ds(pl.multiple_of(peer * share, share), share)],
            dst_ref=hxr.at[i, d - 1], send_sem=hx_send.at[i, d - 1], recv_sem=hx_recv.at[i, d - 1],
            device_id={"seg": peer}, device_id_type=MESH,
        )

    def hz_copy(i, place_in):
        return pltpu.make_async_remote_copy(
            src_ref=hz.at[i],
            dst_ref=hred.at[i % held, :, :, pl.ds(pl.multiple_of(place_in * share, share), share)],
            send_sem=hz_send.at[i], recv_sem=hz_recv.at[i, place_in],
            device_id={"chan": z - 1, "seg": i // held, "freq": s_me // mates}, device_id_type=MESH,
        )

    def hd_copy(i, giver, q):
        return pltpu.make_async_remote_copy(
            src_ref=hbuf.at[i, :, :, q * half : (q + 1) * half],
            dst_ref=hdir.at[i % held, giver], send_sem=hd_send.at[i, q], recv_sem=hd_recv.at[i, giver],
            device_id={"chan": z - 1, "seg": i // held, "freq": q}, device_id_type=MESH,
        )

    def f_copy(i):
        return pltpu.make_async_remote_copy(
            src_ref=fsend.at[i], dst_ref=frecv.at[i], send_sem=f_send.at[i], recv_sem=f_recv.at[i],
            device_id={"freq": twin}, device_id_type=MESH,
        )

    def s_copy(i, slot):
        return pltpu.make_async_remote_copy(
            src_ref=vsum.at[i], dst_ref=srecv.at[i % held, slot],
            send_sem=s_send.at[i], recv_sem=s_recv.at[i, slot],
            device_id={"seg": i // held}, device_id_type=MESH,
        )

    def process(i):
        rows_i = slice(i * R, (i + 1) * R)

        @pl.when(has_src)
        def _():
            last_copy(i).wait_recv()

        chosen = jnp.concatenate([sel[k * W + i * R : k * W + (i + 1) * R, :] for k in range(slots)], axis=0)

        def pieces(s):
            at = slice(s * R, (s + 1) * R)
            blocks = [own_last[b, at, :] for b in range(BLOCKS)]
            blocks += [recv_last[b, at, :] for b in range(i + 1)]
            mine, theirs = blocks[i], blocks[-1]
            blocks += [jnp.zeros((R, 2 * W), BF16)] * (BLOCKS - 1 - i)
            return mine, theirs, jnp.concatenate(blocks, axis=0)

        cross = jnp.concatenate(products(pieces, chosen, i * R, R), axis=0)
        last = dot(cross, dly[chunks - 1])
        for k in range(slots):
            sums = total[k, rows_i, :] + last[k * R : (k + 1) * R]
            other = below(k, i * R, R, LAGS)
            hbuf[i, k] = jnp.where(other, sums, 0.0).astype(BF16)
            total[k, rows_i, :] = jnp.where(other, 0.0, sums)

        @pl.when(sends_h)
        def _():
            if i in DIRECT:
                for q in range(2):
                    hd_copy(i, s_me, q).start()
            else:
                for d in range(1, ns):
                    hx_copy(i, d).start()

        for k in range(slots):
            fsend[i, k] = total[k, rows_i, given].astype(BF16)
        f_copy(i).start()

    def join(i):
        rows_i = slice(i * R, (i + 1) * R)
        f_copy(i).wait_recv()
        for k in range(slots):
            merged = total[k, rows_i, kept] + frecv[i, k].astype(F32)
            total[k, rows_i, kept] = merged
            vsum[i, k] = merged.astype(BF16)

        @pl.when(s_me != i // held)
        def _():
            s_copy(i, lax.rem(s_me - i // held + ns, ns) - 1).start()

    def give_back(i):
        @pl.when(sends_h)
        def _():
            mine = pl.ds(pl.multiple_of(s_me * share, share), share)
            for d in range(1, ns):
                hx_copy(i, d).wait_recv()
            for k in range(slots):
                sums = hbuf[i, k, :, mine].astype(F32)
                for d in range(1, ns):
                    sums += hxr[i, d - 1, k].astype(F32)
                hz[i, k] = sums.astype(BF16)
            hz_copy(i, lax.rem(s_me, mates)).start()

    lax.fori_loop(0, chunks - 1, correlate, 0)
    reduced = [i for i in range(BLOCKS) if i not in DIRECT]
    for i in range(BLOCKS):
        process(i)
        if i > 0:
            join(i - 1)
    for i in reduced[:1]:
        give_back(i)
    join(BLOCKS - 1)
    for i in reduced[1:]:
        give_back(i)

    for i in range(BLOCKS):
        rows_i = slice(i * R, (i + 1) * R)
        j = i % held

        @pl.when(s_me == i // held)
        def _():
            for d in range(1, ns):
                s_copy(i, d - 1).wait_recv()

            @pl.when(takes_h)
            def _():
                if i in DIRECT:
                    for e in range(ns):
                        hd_copy(i, e, 0).wait_recv()
                else:
                    for e in range(mates):
                        hz_copy(i, e).wait_recv()

            for k in range(slots):
                result = total[k, rows_i, kept]
                for d in range(1, ns):
                    result += srecv[j, d - 1, k].astype(F32)
                if i in DIRECT:
                    for e in range(ns):
                        result += hdir[j, e, k].astype(F32)
                else:
                    result += hred[j, k].astype(F32)
                scale = inverse[k, rows_i, :]
                out[j * R : (j + 1) * R, k, :] = result * jnp.concatenate([scale] * (half // W), axis=1)

    @pl.when(has_dst)
    def _():
        def drain(q, carry):
            white_copy(q, whole).wait_send()
            return carry

        lax.fori_loop(0, chunks - 1, drain, 0)
        for i in range(BLOCKS):
            last_copy(i).wait_send()

    @pl.when(z > 0)
    def _():
        count_copy.wait_send()

    @pl.when(sends_h)
    def _():
        for i in range(BLOCKS):
            if i in DIRECT:
                for q in range(2):
                    hd_copy(i, s_me, q).wait_send()
            else:
                for d in range(1, ns):
                    hx_copy(i, d).wait_send()
                hz_copy(i, lax.rem(s_me, mates)).wait_send()

    for s in range(segs):
        power_copy(s).wait_send()
    for i in range(BLOCKS):
        f_copy(i).wait_send()

        @pl.when(s_me != i // held)
        def _():
            s_copy(i, lax.rem(s_me - i // held + ns, ns) - 1).wait_send()


def pin(x):
    return pltpu.with_memory_space_constraint(x, pltpu.HBM)


def shards(traces, dead_mask, seg_counts, offsets):
    segs, chans, length = traces.shape
    nz, ns = lax.axis_size("chan"), lax.axis_size("seg")
    slots = offsets.shape[0]
    chunks = F // 2 // W
    rows = segs * chans
    per = chans // ns
    half = LAGS // 2
    vmem = pl.BlockSpec(memory_space=pltpu.VMEM)
    hbm = pl.BlockSpec(memory_space=pltpu.HBM)
    dma = pltpu.SemaphoreType.DMA
    terms = pl.pallas_call(
        functools.partial(kernel, nz, ns, segs, chunks, slots),
        out_shape=jax.ShapeDtypeStruct((per, slots, half), F32),
        in_specs=[hbm] * 6,
        out_specs=vmem,
        scratch_shapes=[
            pltpu.SMEM((slots,), jnp.int32),
            pltpu.VMEM((1, chans), jnp.int32),
            pltpu.VMEM((1, chans), jnp.int32),
            pltpu.VMEM((rows, length), BF16),
            pltpu.VMEM((1, chans), jnp.int32),
            pltpu.VMEM((slots, W, W), F32),
            pltpu.VMEM((chunks // 4, 4, length // 4, 2 * W), BF16),
            pltpu.VMEM((chunks, 2 * W, LAGS), BF16),
            pltpu.VMEM((4, 2 * W, length // 4), BF16),
            pltpu.VMEM((W, W), F32),
            pltpu.VMEM((6 * W, 2 * W), BF16),
            pltpu.VMEM((chunks, rows, 2 * W), F32),
            pltpu.VMEM((chunks // 2, rows, 2 * W), BF16),
            pltpu.VMEM((rows, 2 * W), BF16),
            pltpu.VMEM((chunks - 1, rows, 2 * W), BF16),
            pltpu.VMEM((chunks - 1, rows, 2 * W), BF16),
            pltpu.VMEM((BLOCKS, segs * R, 2 * W), BF16),
            pltpu.VMEM((BLOCKS, segs * R, 2 * W), BF16),
            pltpu.VMEM((slots * W, 2 * W), BF16),
            pltpu.VMEM((rows, W), F32),
            pltpu.VMEM((slots, W, LAGS), F32),
            pltpu.VMEM((BLOCKS, slots, R, LAGS), BF16),
            pltpu.VMEM((BLOCKS, ns - 1, slots, R, LAGS // ns), BF16),
            pltpu.VMEM((BLOCKS, slots, R, LAGS // ns), BF16),
            pltpu.VMEM((BLOCKS // ns, slots, R, half), BF16),
            pltpu.VMEM((BLOCKS // ns, ns, slots, R, half), BF16),
            pltpu.VMEM((BLOCKS, slots, R, half), BF16),
            pltpu.VMEM((BLOCKS, slots, R, half), BF16),
            pltpu.VMEM((BLOCKS, slots, R, half), BF16),
            pltpu.VMEM((BLOCKS // ns, ns - 1, slots, R, half), BF16),
            dma((3,)),
            dma((segs,)),
            dma,
            dma,
            dma((chunks // 4,)),
            dma,
            dma((segs,)),
            dma((segs,)),
            dma((chunks - 1,)),
            dma((chunks - 1,)),
            dma((BLOCKS,)),
            dma((BLOCKS,)),
            dma((BLOCKS, ns - 1)),
            dma((BLOCKS, ns - 1)),
            dma((BLOCKS,)),
            dma((BLOCKS, ns // 2)),
            dma((BLOCKS, 2)),
            dma((BLOCKS, ns)),
            dma((BLOCKS,)),
            dma((BLOCKS,)),
            dma((BLOCKS,)),
            dma((BLOCKS, ns - 1)),
        ],
        compiler_params=pltpu.CompilerParams(
            collective_id=0, has_side_effects=True, vmem_limit_bytes=50 * 1024 * 1024
        ),
    )(
        pin(offsets),
        pin(traces.reshape(rows, length)),
        pin(dead_mask.reshape(1, chans)),
        pin(seg_counts.reshape(1, chans)),
        jnp.asarray(fourier_blocks(length)),
        jnp.asarray(delay_blocks(length, chunks)),
    )
    return terms


def solution(mesh):
    in_specs = (
        P("seg", ("groups", "chan"), None),
        P(("groups", "chan")),
        P(("groups", "chan")),
        P(),
    )
    out_specs = P(("groups", "chan", "seg"), None, "freq")
    return jax.shard_map(shards, mesh=mesh, in_specs=in_specs, out_specs=out_specs, check_vma=False)
```

```python
import functools
import math

import jax
import jax.numpy as jnp
import ml_dtypes
import numpy as np
from jax import lax
from jax.experimental import pallas as pl
from jax.experimental.pallas import tpu as pltpu
from jax.sharding import PartitionSpec as P

HALF = 32
LAGS = 512
F = 2048
W = 128
EPS = 1e-06
BLOCKS = 4
LATE = 2
LAG = 2
R = W // BLOCKS
DIRECT = (2, 3)
MESH = pl.DeviceIdType.MESH
F32 = jnp.float32
BF16 = jnp.bfloat16


def bins_of(freq, group, parity):
    m = np.arange(W)
    if freq == 0:
        return 2 * W * group + 2 * m + parity
    return F - 1 - (2 * W * group + 2 * m + 1 - parity)


def fourier_blocks(length):
    quarter = length // 4
    t = np.arange(quarter)[:, None]
    wave = 2.0 * math.pi * np.arange(length) / length
    cos = np.cos(wave).astype(np.float32).astype(ml_dtypes.bfloat16)
    sin = (-np.sin(wave)).astype(np.float32).astype(ml_dtypes.bfloat16)
    groups = F // 2 // (2 * W)
    out = np.empty((2, groups // 2, 4, quarter, 2 * W), ml_dtypes.bfloat16)
    for freq in range(2):
        for h in range(groups // 2):
            for parity in range(2):
                bins = np.concatenate([bins_of(freq, 2 * h + i, parity) for i in range(2)])
                phase = t * bins[None, :] % length
                out[freq, h, 2 * parity] = cos[phase]
                out[freq, h, 2 * parity + 1] = sin[phase]
                if parity == 1:
                    out[freq, h, 3, 0] = sin[quarter * bins % length]
    return out


def delay_blocks(length, chunks):
    shifts = np.arange(LAGS)[None, :] - LAGS // 2
    out = np.empty((2, chunks, 2 * W, LAGS), ml_dtypes.bfloat16)
    for freq in range(2):
        for q in range(chunks):
            phase = bins_of(freq, q // 2, q % 2)[:, None] * shifts % length * (2.0 * math.pi / length)
            out[freq, q, :W] = (np.cos(phase) / math.sqrt(F)).astype(np.float32)
            out[freq, q, W:] = (-np.sin(phase) / math.sqrt(F)).astype(np.float32)
    return out


def dot(a, b):
    return jnp.dot(a, b, preferred_element_type=F32)


def iota(shape, dim):
    return lax.broadcasted_iota(jnp.int32, shape, dim)


def kernel(
    nz, ns, segs, chunks, slots, offs_in, traces, dead_in, cnt_in, four, delay, out,
    offs, dead, cnt,
    tr, crecv, inverse, table, dly, lhs, mid, band, spec, power, near, own, recv, own_last, recv_last, sel, mask, total,
    hbuf, hxr, hz, hred, hdir, fsend, frecv, vsum, srecv,
    in_sem, tr_sem, c_send, c_recv, tab_sem, dly_sem, p_send, p_recv, w_send, w_recv, t_send, t_recv, hx_send, hx_recv, hz_send, hz_recv,
    hd_send, hd_recv, f_send, f_recv, s_send, s_recv,
):
    z = lax.axis_index("chan")
    s_me = lax.axis_index("seg")
    fq = lax.axis_index("freq")
    up = fq == 1
    groups = chunks // 2
    wide = 2 * W
    half_blocks = traces.shape[1] // 2 // wide
    rows = own.shape[1]
    per = W // ns
    step = 2 * fq - 1
    dst = z + step
    src = z - step
    has_dst = jnp.logical_and(dst >= 0, dst < nz)
    has_src = jnp.logical_and(src >= 0, src < nz)
    twin = 1 - fq

    def table_copy(h):
        return pltpu.make_async_copy(four.at[fq, h], table.at[h], tab_sem.at[h])

    def trace_copy(s):
        return pltpu.make_async_copy(
            traces.at[pl.ds(s * W, W)], tr.at[pl.ds(s * W, W)], tr_sem.at[s]
        )

    small = [
        pltpu.make_async_copy(a, b, in_sem.at[i])
        for i, (a, b) in enumerate(((offs_in, offs), (dead_in, dead), (cnt_in, cnt)))
    ]
    for copy in small:
        copy.start()
    trace_copy(0).start()
    for h in range(groups // 2):
        table_copy(h).start()
    for s in range(1, segs):
        trace_copy(s).start()
    delay_copy = pltpu.make_async_copy(delay.at[fq], dly, dly_sem)
    delay_copy.start()

    sends_h = jnp.logical_and(up, z > 0)
    takes_h = z < nz - 1
    barrier = pltpu.get_barrier_semaphore()

    @pl.when(has_src)
    def _():
        pl.semaphore_signal(barrier, inc=1, device_id={"chan": src}, device_id_type=MESH)

    pl.semaphore_signal(barrier, inc=1, device_id={"freq": twin}, device_id_type=MESH)
    for d in range(1, ns):
        pl.semaphore_signal(
            barrier, inc=1, device_id={"seg": lax.rem(s_me + d, ns)}, device_id_type=MESH
        )

    @pl.when(takes_h)
    def _():
        for d in range(ns):
            giver = {"chan": z + 1, "seg": lax.rem(s_me + d, ns), "freq": 1}
            pl.semaphore_signal(barrier, inc=1, device_id=giver, device_id_type=MESH)

    for copy in small:
        copy.wait()
    diag = iota((W, W), 0) == iota((W, W), 1)
    cnt_col = jnp.sum(jnp.where(diag, cnt[...], 0).astype(F32), axis=1, keepdims=True)
    live_col = jnp.sum(jnp.where(diag, dead[...], 0).astype(F32), axis=1, keepdims=True)
    for s in range(segs):
        seg_number = (s_me * segs + s).astype(F32)
        valid = jnp.where(seg_number < cnt_col, live_col, 0.0)
        mask[s * W : (s + 1) * W, :] = jnp.broadcast_to(valid, (W, W))
    turn = 2 * W - 1 - W * fq
    for k in range(slots):
        target = (iota((W, 2 * W), 0) + offs[k]) & turn
        sel[k * W : (k + 1) * W, :] = jnp.where(iota((W, 2 * W), 1) == target, 1.0, 0.0).astype(BF16)

    @pl.when(jnp.logical_not(takes_h))
    def _():
        hred[...] = jnp.zeros_like(hred)
        hdir[...] = jnp.zeros_like(hdir)
        crecv[...] = jnp.zeros_like(crecv)

    alternate = (1 - 2 * (iota((1, W), 1) & 1)).astype(F32) * (1 - 2 * fq).astype(F32)

    def place(lane, core):
        return 2 * (lane & (W - 1)) + ((lane >> 7) ^ core)

    row_lane = iota((wide, wide), 0)
    col = place(iota((wide, wide), 1), fq)
    inside = place(row_lane, fq)
    around = inside + jnp.where((row_lane & (W - 1)) < W // 2, wide, -wide)
    across = 2 * wide - 1 - place(row_lane, twin)
    for i, at in enumerate((inside, around, across)):
        band[i * wide : (i + 1) * wide, :] = jnp.where(jnp.abs(at - col) <= HALF, 1.0, 0.0).astype(BF16)
    flip = jnp.where(iota((wide, wide), 0) + iota((wide, wide), 1) == wide, 1.0, 0.0).astype(BF16)
    first_lane = iota((W, W), 1) == 0
    low_lane = (iota((1, wide), 1) & (W - 1)) < W // 2

    def at_first(new, old):
        return jnp.concatenate([jnp.where(first_lane, new[:, :W], old[:, :W]), old[:, W:]], axis=1)

    def fold(at):
        def x(j):
            return tr[at, j * wide : (j + 1) * wide]

        quads = half_blocks // 2
        back = dot(
            jnp.concatenate(
                [x(half_blocks - 1 - j) for j in range(quads)]
                + [x(2 * half_blocks - 1 - j) for j in range(quads)],
                axis=0,
            ),
            flip,
        )
        for j in range(quads):
            a = x(j).astype(F32)
            b = x(half_blocks + j).astype(F32)
            a_back = back[j * W : (j + 1) * W]
            b_back = back[(quads + j) * W : (quads + j + 1) * W]
            if j > 0:
                a_back = at_first(x(half_blocks - j).astype(F32), a_back)
                b_back = at_first(x(2 * half_blocks - j).astype(F32), b_back)
            even, odd = a + b, a - b
            even_back, odd_back = a_back + b_back, a_back - b_back
            odd_sin = odd + odd_back
            if j == 0:
                a_mid = x(quads).astype(F32)
                b_mid = x(half_blocks + quads).astype(F32)
                odd_sin = at_first(a_mid - b_mid, odd_sin)
                mid[...] = (a_mid + b_mid)[:, :1] * alternate
            for i, term in enumerate((even + even_back, even - even_back, odd - odd_back, odd_sin)):
                high = term.astype(BF16)
                lhs[i, :W, j * wide : (j + 1) * wide] = high
                lhs[i, W:, j * wide : (j + 1) * wide] = (term - high.astype(F32)).astype(BF16)

    def transform(h, at):
        def part(i):
            both = dot(lhs[i], table[h, i])
            return both[:W] + both[W:]

        middle = mid[...]
        for parity in range(2):
            re = part(2 * parity)
            im = part(2 * parity + 1)
            if parity == 0:
                re = re + jnp.concatenate([middle, middle], axis=1)
            square = (re * re + im * im).astype(BF16)
            for i in range(2):
                lanes = slice(i * W, (i + 1) * W)
                spec[4 * h + 2 * i + parity, at, :W] = re[:, lanes]
                spec[4 * h + 2 * i + parity, at, W:] = im[:, lanes]
                power[2 * h + i, at, parity * W : (parity + 1) * W] = square[:, lanes]

    def whiten(g, s, factors):
        at = rows_of(s)
        around = jnp.where(
            low_lane,
            power[g + 1, at, :] if g + 1 < groups else jnp.zeros((), BF16),
            power[g - 1, at, :] if g > 0 else jnp.zeros((), BF16),
        )
        parts = [power[g, at, :], around]
        if g + 1 == groups:
            parts.append(near[at, :])
        window = dot(jnp.concatenate(parts, axis=1), band[: len(parts) * wide, :])
        u = g * wide + place(iota((1, wide), 1), fq)
        number = (jnp.minimum(u, HALF) + HALF + 1).astype(F32)
        factor = jnp.concatenate([factors, factors], axis=1) * lax.rsqrt(window / number + EPS)
        for parity in range(2):
            scale = factor[:, parity * W : (parity + 1) * W]
            q = 2 * g + parity
            re = (spec[q, at, :W] * scale).astype(BF16)
            im = (spec[q, at, W:] * scale).astype(BF16)
            if q + LATE < chunks:
                own[q, at, :W] = re
                own[q, at, W:] = im
            else:
                for i in range(BLOCKS):
                    to = pl.ds(pl.multiple_of(s * R, R), R)
                    own_last[i, q + LATE - chunks, to, :W] = re[i * R : (i + 1) * R]
                    own_last[i, q + LATE - chunks, to, W:] = im[i * R : (i + 1) * R]

    def power_copy(s):
        return pltpu.make_async_remote_copy(
            src_ref=power.at[groups - 1, rows_of(s)], dst_ref=near.at[rows_of(s)],
            send_sem=p_send.at[s], recv_sem=p_recv.at[s],
            device_id={"freq": twin}, device_id_type=MESH,
        )

    def white_copy(q, at):
        return pltpu.make_async_remote_copy(
            src_ref=own.at[q, at], dst_ref=recv.at[q, at],
            send_sem=w_send.at[q], recv_sem=w_recv.at[q],
            device_id={"chan": dst}, device_id_type=MESH,
        )

    def last_copy(i):
        return pltpu.make_async_remote_copy(
            src_ref=own_last.at[i], dst_ref=recv_last.at[i],
            send_sem=t_send.at[i], recv_sem=t_recv.at[i],
            device_id={"chan": dst}, device_id_type=MESH,
        )

    def send(q, at):
        @pl.when(has_dst)
        def _():
            white_copy(q, at).start()

    whole = pl.ds(0, rows)

    def rows_of(s):
        return pl.ds(pl.multiple_of(s * W, W), W)

    count_copy = pltpu.make_async_remote_copy(
        src_ref=cnt, dst_ref=crecv, send_sem=c_send, recv_sem=c_recv,
        device_id={"chan": z - 1}, device_id_type=MESH,
    )
    peers = ns + has_dst.astype(jnp.int32) + 2 * ns * sends_h.astype(jnp.int32)

    def segment(s, first):
        at = rows_of(s)
        trace_copy(s).wait()
        fold(at)
        if first:
            table_copy(0).wait()
        transform(0, at)
        whiten_rows = mask[at, :]
        whiten(0, s, whiten_rows)
        if first:
            pl.semaphore_wait(barrier, peers)

            @pl.when(z > 0)
            def _():
                count_copy.start()

        send(0, at)
        send(1, at)
        for h in range(1, groups // 2):
            if first:
                table_copy(h).wait()
            transform(h, at)
        power_copy(s).start()
        whiten(1, s, whiten_rows)
        send(2, at)
        send(3, at)

    segment(0, True)

    def later(s, carry):
        segment(s, False)
        return carry

    lax.fori_loop(1, segs, later, 0)

    def finish(g, s):
        whiten(g, s, mask[rows_of(s), :])

    for g in range(2, groups):
        def each(s, carry, g=g):
            if g + 1 == groups:
                power_copy(s).wait_recv()
            finish(g, s)
            return carry

        lax.fori_loop(0, segs, each, 0)
        for q in (2 * g, 2 * g + 1):
            if q + LATE < chunks:
                send(q, whole)

    @pl.when(has_dst)
    def _():
        for i in range(BLOCKS):
            last_copy(i).start()

    @pl.when(jnp.logical_not(has_src))
    def _():
        def clear(q, carry):
            recv[q] = jnp.zeros((rows, 2 * W), BF16)
            return carry

        lax.fori_loop(0, chunks - LATE, clear, 0)
        recv_last[...] = jnp.zeros_like(recv_last)

    delay_copy.wait()
    total[...] = jnp.zeros_like(total)

    @pl.when(takes_h)
    def _():
        count_copy.wait_recv()

    counts = jnp.concatenate([cnt[...], crecv[...]], axis=1)
    for k in range(slots):
        partner = jnp.where(iota((W, 2 * W), 1) == iota((W, 2 * W), 0) + offs[k], counts, 0).astype(F32)
        fewer = jnp.minimum(cnt_col, jnp.sum(partner, axis=1, keepdims=True))
        inverse[k] = jnp.broadcast_to(1.0 / jnp.maximum(fewer, 1.0), (W, W))

    def below(k, first, number, width):
        return jnp.logical_and(iota((number, width), 0) + (offs[k] + first) >= W, up)

    def products(pieces, chosen, first, number):
        re = [None] * slots
        im = [None] * slots
        for s in range(segs):
            mine, theirs, both = pieces(s)
            pair = dot(chosen, both)
            mine = mine.astype(F32)
            theirs = theirs.astype(F32)
            for k in range(slots):
                other = below(k, first, number, W)
                my_re = jnp.where(other, theirs[:, :W], mine[:, :W])
                my_im = jnp.where(other, theirs[:, W:], mine[:, W:])
                pair_re = pair[k * number : (k + 1) * number, :W]
                pair_im = pair[k * number : (k + 1) * number, W:]
                one = my_re * pair_re + my_im * pair_im
                two = my_im * pair_re - my_re * pair_im
                re[k] = one if s == 0 else re[k] + one
                im[k] = two if s == 0 else im[k] + two
        return [jnp.concatenate([a, b], axis=1).astype(BF16) for a, b in zip(re, im)]

    def correlate(q, carry):
        @pl.when(has_src)
        def _():
            white_copy(q, whole).wait_recv()

        def pieces(s):
            at = slice(s * W, (s + 1) * W)
            mine, theirs = own[q, at, :], recv[q, at, :]
            return mine, theirs, jnp.concatenate([mine, theirs], axis=0)

        for k, cross in enumerate(products(pieces, sel[...], 0, W)):
            total[k] += dot(cross, dly[q])
        return carry

    half = LAGS // 2
    kept = pl.ds(pl.multiple_of(fq * half, half), half)
    given = pl.ds(pl.multiple_of(twin * half, half), half)
    held = BLOCKS // ns
    share = LAGS // ns
    mates = ns // 2

    def share_of(s):
        return pl.ds(pl.multiple_of(lax.rem(s, mates) * share, share), share)

    def hx_copy(i, d):
        peer = lax.rem(s_me + d, ns)
        return pltpu.make_async_remote_copy(
            src_ref=hbuf.at[i, peer // mates, :, :, share_of(peer)],
            dst_ref=hxr.at[i, d - 1], send_sem=hx_send.at[i, d - 1], recv_sem=hx_recv.at[i, d - 1],
            device_id={"seg": peer}, device_id_type=MESH,
        )

    def hz_copy(i, place_in):
        return pltpu.make_async_remote_copy(
            src_ref=hz.at[i],
            dst_ref=hred.at[i % held, :, :, pl.ds(pl.multiple_of(place_in * share, share), share)],
            send_sem=hz_send.at[i], recv_sem=hz_recv.at[i, place_in],
            device_id={"chan": z - 1, "seg": i // held, "freq": s_me // mates}, device_id_type=MESH,
        )

    def hd_copy(i, giver, q):
        return pltpu.make_async_remote_copy(
            src_ref=hbuf.at[i, q],
            dst_ref=hdir.at[i % held, giver], send_sem=hd_send.at[i, q], recv_sem=hd_recv.at[i, giver],
            device_id={"chan": z - 1, "seg": i // held, "freq": q}, device_id_type=MESH,
        )

    def f_copy(i):
        return pltpu.make_async_remote_copy(
            src_ref=fsend.at[i], dst_ref=frecv.at[i], send_sem=f_send.at[i], recv_sem=f_recv.at[i],
            device_id={"freq": twin}, device_id_type=MESH,
        )

    def s_copy(i, slot):
        return pltpu.make_async_remote_copy(
            src_ref=vsum.at[i], dst_ref=srecv.at[i % held, slot],
            send_sem=s_send.at[i], recv_sem=s_recv.at[i, slot],
            device_id={"seg": i // held}, device_id_type=MESH,
        )

    def process(i):
        rows_i = slice(i * R, (i + 1) * R)

        @pl.when(has_src)
        def _():
            last_copy(i).wait_recv()

        chosen = jnp.concatenate([sel[k * W + i * R : k * W + (i + 1) * R, :] for k in range(slots)], axis=0)

        def pieces(p, s):
            at = slice(s * R, (s + 1) * R)
            blocks = [own_last[b, p, at, :] for b in range(BLOCKS)]
            blocks += [recv_last[b, p, at, :] for b in range(i + 1)]
            mine, theirs = blocks[i], blocks[-1]
            blocks += [jnp.zeros((R, 2 * W), BF16)] * (BLOCKS - 1 - i)
            return mine, theirs, jnp.concatenate(blocks, axis=0)

        last = 0.0
        for p in range(LATE):
            cross = jnp.concatenate(products(functools.partial(pieces, p), chosen, i * R, R), axis=0)
            last = last + dot(cross, dly[chunks - LATE + p])
        for k in range(slots):
            sums = total[k, rows_i, :] + last[k * R : (k + 1) * R]
            other = below(k, i * R, R, LAGS)
            returned = jnp.where(other, sums, 0.0).astype(BF16)
            for q in range(2):
                hbuf[i, q, k] = returned[:, q * half : (q + 1) * half]
            total[k, rows_i, :] = jnp.where(other, 0.0, sums)

        @pl.when(sends_h)
        def _():
            if i in DIRECT:
                for q in range(2):
                    hd_copy(i, s_me, q).start()
            else:
                for d in range(1, ns):
                    hx_copy(i, d).start()

        for k in range(slots):
            fsend[i, k] = total[k, rows_i, given].astype(BF16)
        f_copy(i).start()

    def join(i):
        rows_i = slice(i * R, (i + 1) * R)
        f_copy(i).wait_recv()
        for k in range(slots):
            merged = total[k, rows_i, kept] + frecv[i, k].astype(F32)
            total[k, rows_i, kept] = merged
            vsum[i, k] = merged.astype(BF16)

        @pl.when(s_me != i // held)
        def _():
            s_copy(i, lax.rem(s_me - i // held + ns, ns) - 1).start()

    def give_back(i):
        @pl.when(sends_h)
        def _():
            for d in range(1, ns):
                hx_copy(i, d).wait_recv()
            for k in range(slots):
                sums = hbuf[i, s_me // mates, k, :, share_of(s_me)].astype(F32)
                for d in range(1, ns):
                    sums += hxr[i, d - 1, k].astype(F32)
                hz[i, k] = sums.astype(BF16)
            hz_copy(i, lax.rem(s_me, mates)).start()

    lax.fori_loop(0, chunks - LATE, correlate, 0)
    reduced = [i for i in range(BLOCKS) if i not in DIRECT]
    for i in range(BLOCKS):
        process(i)
        if i > 0:
            join(i - 1)
        if i >= LAG and i - LAG in reduced:
            give_back(i - LAG)
    join(BLOCKS - 1)
    for i in reduced:
        if i + LAG >= BLOCKS:
            give_back(i)

    for i in range(BLOCKS):
        rows_i = slice(i * R, (i + 1) * R)
        j = i % held

        @pl.when(s_me == i // held)
        def _():
            for d in range(1, ns):
                s_copy(i, d - 1).wait_recv()

            @pl.when(takes_h)
            def _():
                if i in DIRECT:
                    for e in range(ns):
                        hd_copy(i, e, 0).wait_recv()
                else:
                    for e in range(mates):
                        hz_copy(i, e).wait_recv()

            for k in range(slots):
                result = total[k, rows_i, kept]
                for d in range(1, ns):
                    result += srecv[j, d - 1, k].astype(F32)
                if i in DIRECT:
                    for e in range(ns):
                        result += hdir[j, e, k].astype(F32)
                else:
                    result += hred[j, k].astype(F32)
                scale = inverse[k, rows_i, :]
                out[j * R : (j + 1) * R, k, :] = result * jnp.concatenate([scale] * (half // W), axis=1)

    @pl.when(has_dst)
    def _():
        def drain(q, carry):
            white_copy(q, whole).wait_send()
            return carry

        lax.fori_loop(0, chunks - LATE, drain, 0)
        for i in range(BLOCKS):
            last_copy(i).wait_send()

    @pl.when(z > 0)
    def _():
        count_copy.wait_send()

    @pl.when(sends_h)
    def _():
        for i in range(BLOCKS):
            if i in DIRECT:
                for q in range(2):
                    hd_copy(i, s_me, q).wait_send()
            else:
                for d in range(1, ns):
                    hx_copy(i, d).wait_send()
                hz_copy(i, lax.rem(s_me, mates)).wait_send()

    for s in range(segs):
        power_copy(s).wait_send()
    for i in range(BLOCKS):
        f_copy(i).wait_send()

        @pl.when(s_me != i // held)
        def _():
            s_copy(i, lax.rem(s_me - i // held + ns, ns) - 1).wait_send()


def pin(x):
    return pltpu.with_memory_space_constraint(x, pltpu.HBM)


def shards(traces, dead_mask, seg_counts, offsets):
    segs, chans, length = traces.shape
    nz, ns = lax.axis_size("chan"), lax.axis_size("seg")
    slots = offsets.shape[0]
    chunks = F // 2 // W
    rows = segs * chans
    per = chans // ns
    half = LAGS // 2
    vmem = pl.BlockSpec(memory_space=pltpu.VMEM)
    hbm = pl.BlockSpec(memory_space=pltpu.HBM)
    dma = pltpu.SemaphoreType.DMA
    terms = pl.pallas_call(
        functools.partial(kernel, nz, ns, segs, chunks, slots),
        out_shape=jax.ShapeDtypeStruct((per, slots, half), F32),
        in_specs=[hbm] * 6,
        out_specs=vmem,
        scratch_shapes=[
            pltpu.SMEM((slots,), jnp.int32),
            pltpu.VMEM((1, chans), jnp.int32),
            pltpu.VMEM((1, chans), jnp.int32),
            pltpu.VMEM((rows, length), BF16),
            pltpu.VMEM((1, chans), jnp.int32),
            pltpu.VMEM((slots, W, W), F32),
            pltpu.VMEM((chunks // 4, 4, length // 4, 2 * W), BF16),
            pltpu.VMEM((chunks, 2 * W, LAGS), BF16),
            pltpu.VMEM((4, 2 * W, length // 4), BF16),
            pltpu.VMEM((W, W), F32),
            pltpu.VMEM((6 * W, 2 * W), BF16),
            pltpu.VMEM((chunks, rows, 2 * W), F32),
            pltpu.VMEM((chunks // 2, rows, 2 * W), BF16),
            pltpu.VMEM((rows, 2 * W), BF16),
            pltpu.VMEM((chunks - LATE, rows, 2 * W), BF16),
            pltpu.VMEM((chunks - LATE, rows, 2 * W), BF16),
            pltpu.VMEM((BLOCKS, LATE, segs * R, 2 * W), BF16),
            pltpu.VMEM((BLOCKS, LATE, segs * R, 2 * W), BF16),
            pltpu.VMEM((slots * W, 2 * W), BF16),
            pltpu.VMEM((rows, W), F32),
            pltpu.VMEM((slots, W, LAGS), F32),
            pltpu.VMEM((BLOCKS, 2, slots, R, half), BF16),
            pltpu.VMEM((BLOCKS, ns - 1, slots, R, LAGS // ns), BF16),
            pltpu.VMEM((BLOCKS, slots, R, LAGS // ns), BF16),
            pltpu.VMEM((BLOCKS // ns, slots, R, half), BF16),
            pltpu.VMEM((BLOCKS // ns, ns, slots, R, half), BF16),
            pltpu.VMEM((BLOCKS, slots, R, half), BF16),
            pltpu.VMEM((BLOCKS, slots, R, half), BF16),
            pltpu.VMEM((BLOCKS, slots, R, half), BF16),
            pltpu.VMEM((BLOCKS // ns, ns - 1, slots, R, half), BF16),
            dma((3,)),
            dma((segs,)),
            dma,
            dma,
            dma((chunks // 4,)),
            dma,
            dma((segs,)),
            dma((segs,)),
            dma((chunks - LATE,)),
            dma((chunks - LATE,)),
            dma((BLOCKS,)),
            dma((BLOCKS,)),
            dma((BLOCKS, ns - 1)),
            dma((BLOCKS, ns - 1)),
            dma((BLOCKS,)),
            dma((BLOCKS, ns // 2)),
            dma((BLOCKS, 2)),
            dma((BLOCKS, ns)),
            dma((BLOCKS,)),
            dma((BLOCKS,)),
            dma((BLOCKS,)),
            dma((BLOCKS, ns - 1)),
        ],
        compiler_params=pltpu.CompilerParams(
            collective_id=0, has_side_effects=True, vmem_limit_bytes=50 * 1024 * 1024
        ),
    )(
        pin(offsets),
        pin(traces.reshape(rows, length)),
        pin(dead_mask.reshape(1, chans)),
        pin(seg_counts.reshape(1, chans)),
        jnp.asarray(fourier_blocks(length)),
        jnp.asarray(delay_blocks(length, chunks)),
    )
    return terms


def solution(mesh):
    in_specs = (
        P("seg", ("groups", "chan"), None),
        P(("groups", "chan")),
        P(("groups", "chan")),
        P(),
    )
    out_specs = P(("groups", "chan", "seg"), None, "freq")
    return jax.shard_map(shards, mesh=mesh, in_specs=in_specs, out_specs=out_specs, check_vma=False)
```

```python
import functools
import math

import jax
import jax.numpy as jnp
import ml_dtypes
import numpy as np
from jax import lax
from jax.experimental import pallas as pl
from jax.experimental.pallas import tpu as pltpu
from jax.sharding import PartitionSpec as P

HALF = 32
LAGS = 512
F = 2048
W = 128
EPS = 1e-06
BLOCKS = 4
LATE = 2
LAG = 2
R = W // BLOCKS
DIRECT = (2, 3)
MESH = pl.DeviceIdType.MESH
F32 = jnp.float32
BF16 = jnp.bfloat16


def bins_of(freq, group, parity):
    m = np.arange(W)
    if freq == 0:
        return 2 * W * group + 2 * m + parity
    return F - 1 - (2 * W * group + 2 * m + 1 - parity)


def fourier_blocks(length):
    quarter = length // 4
    t = np.arange(quarter)[:, None]
    wave = 2.0 * math.pi * np.arange(length) / length
    cos = np.cos(wave).astype(np.float32).astype(ml_dtypes.bfloat16)
    sin = (-np.sin(wave)).astype(np.float32).astype(ml_dtypes.bfloat16)
    groups = F // 2 // (2 * W)
    out = np.empty((2, groups // 2, 4, quarter, 2 * W), ml_dtypes.bfloat16)
    for freq in range(2):
        for h in range(groups // 2):
            for parity in range(2):
                bins = np.concatenate([bins_of(freq, 2 * h + i, parity) for i in range(2)])
                phase = t * bins[None, :] % length
                out[freq, h, 2 * parity] = cos[phase]
                out[freq, h, 2 * parity + 1] = sin[phase]
                if parity == 1:
                    out[freq, h, 3, 0] = sin[quarter * bins % length]
    return out


def delay_blocks(length, chunks):
    shifts = np.arange(LAGS)[None, :] - LAGS // 2
    out = np.empty((2, chunks, 2 * W, LAGS), ml_dtypes.bfloat16)
    for freq in range(2):
        for q in range(chunks):
            phase = bins_of(freq, q // 2, q % 2)[:, None] * shifts % length * (2.0 * math.pi / length)
            out[freq, q, :W] = (np.cos(phase) / math.sqrt(F)).astype(np.float32)
            out[freq, q, W:] = (-np.sin(phase) / math.sqrt(F)).astype(np.float32)
    return out


def dot(a, b):
    return jnp.dot(a, b, preferred_element_type=F32)


def iota(shape, dim):
    return lax.broadcasted_iota(jnp.int32, shape, dim)


def kernel(
    nz, ns, segs, chunks, slots, offs_in, traces, dead_in, cnt_in, four, delay, out,
    offs, dead, cnt,
    tr, crecv, inverse, table, dly, lhs, mid, band, spec, power, near, own, recv, own_last, recv_last, sel, mask, total,
    hbuf, hxr, hz, hred, hdir, fsend, frecv, vsum, srecv,
    in_sem, tr_sem, c_send, c_recv, tab_sem, dly_sem, p_send, p_recv, w_send, w_recv, t_send, t_recv, hx_send, hx_recv, hz_send, hz_recv,
    hd_send, hd_recv, f_send, f_recv, s_send, s_recv,
):
    z = lax.axis_index("chan")
    s_me = lax.axis_index("seg")
    fq = lax.axis_index("freq")
    up = fq == 1
    groups = chunks // 2
    wide = 2 * W
    half_blocks = traces.shape[1] // 2 // wide
    rows = own.shape[1]
    per = W // ns
    step = 2 * fq - 1
    dst = z + step
    src = z - step
    has_dst = jnp.logical_and(dst >= 0, dst < nz)
    has_src = jnp.logical_and(src >= 0, src < nz)
    twin = 1 - fq

    def table_copy(h):
        return pltpu.make_async_copy(four.at[fq, h], table.at[h], tab_sem.at[h])

    def trace_copy(s):
        return pltpu.make_async_copy(
            traces.at[pl.ds(s * W, W)], tr.at[pl.ds(s * W, W)], tr_sem.at[s]
        )

    small = [
        pltpu.make_async_copy(a, b, in_sem.at[i])
        for i, (a, b) in enumerate(((offs_in, offs), (dead_in, dead), (cnt_in, cnt)))
    ]
    for copy in small:
        copy.start()
    trace_copy(0).start()
    for h in range(groups // 2):
        table_copy(h).start()
    for s in range(1, segs):
        trace_copy(s).start()
    delay_copy = pltpu.make_async_copy(delay.at[fq], dly, dly_sem)
    delay_copy.start()

    sends_h = jnp.logical_and(up, z > 0)
    takes_h = z < nz - 1
    barrier = pltpu.get_barrier_semaphore()

    @pl.when(has_src)
    def _():
        pl.semaphore_signal(barrier, inc=1, device_id={"chan": src}, device_id_type=MESH)

    pl.semaphore_signal(barrier, inc=1, device_id={"freq": twin}, device_id_type=MESH)
    for d in range(1, ns):
        pl.semaphore_signal(
            barrier, inc=1, device_id={"seg": lax.rem(s_me + d, ns)}, device_id_type=MESH
        )

    @pl.when(takes_h)
    def _():
        for d in range(ns):
            giver = {"chan": z + 1, "seg": lax.rem(s_me + d, ns), "freq": 1}
            pl.semaphore_signal(barrier, inc=1, device_id=giver, device_id_type=MESH)

    for copy in small:
        copy.wait()
    diag = iota((W, W), 0) == iota((W, W), 1)
    cnt_col = jnp.sum(jnp.where(diag, cnt[...], 0).astype(F32), axis=1, keepdims=True)
    live_col = jnp.sum(jnp.where(diag, dead[...], 0).astype(F32), axis=1, keepdims=True)
    for s in range(segs):
        seg_number = (s_me * segs + s).astype(F32)
        valid = jnp.where(seg_number < cnt_col, live_col, 0.0)
        mask[s * W : (s + 1) * W, :] = jnp.broadcast_to(valid, (W, W))
    turn = 2 * W - 1 - W * fq
    for k in range(slots):
        target = (iota((W, 2 * W), 0) + offs[k]) & turn
        sel[k * W : (k + 1) * W, :] = jnp.where(iota((W, 2 * W), 1) == target, 1.0, 0.0).astype(BF16)

    @pl.when(jnp.logical_not(takes_h))
    def _():
        hred[...] = jnp.zeros_like(hred)
        hdir[...] = jnp.zeros_like(hdir)
        crecv[...] = jnp.zeros_like(crecv)

    alternate = (1 - 2 * (iota((1, W), 1) & 1)).astype(F32) * (1 - 2 * fq).astype(F32)

    def place(lane, core):
        return 2 * (lane & (W - 1)) + ((lane >> 7) ^ core)

    row_lane = iota((wide, wide), 0)
    col = place(iota((wide, wide), 1), fq)
    inside = place(row_lane, fq)
    around = inside + jnp.where((row_lane & (W - 1)) < W // 2, wide, -wide)
    across = 2 * wide - 1 - place(row_lane, twin)
    for i, at in enumerate((inside, around, across)):
        band[i * wide : (i + 1) * wide, :] = jnp.where(jnp.abs(at - col) <= HALF, 1.0, 0.0).astype(BF16)
    flip = jnp.where(iota((wide, wide), 0) + iota((wide, wide), 1) == wide, 1.0, 0.0).astype(BF16)
    first_lane = iota((W, W), 1) == 0
    low_lane = (iota((1, wide), 1) & (W - 1)) < W // 2

    def at_first(new, old):
        return jnp.concatenate([jnp.where(first_lane, new[:, :W], old[:, :W]), old[:, W:]], axis=1)

    def fold(at):
        def x(j):
            return tr[at, j * wide : (j + 1) * wide]

        quads = half_blocks // 2
        back = dot(
            jnp.concatenate(
                [x(half_blocks - 1 - j) for j in range(quads)]
                + [x(2 * half_blocks - 1 - j) for j in range(quads)],
                axis=0,
            ),
            flip,
        )
        for j in range(quads):
            a = x(j).astype(F32)
            b = x(half_blocks + j).astype(F32)
            a_back = back[j * W : (j + 1) * W]
            b_back = back[(quads + j) * W : (quads + j + 1) * W]
            if j > 0:
                a_back = at_first(x(half_blocks - j).astype(F32), a_back)
                b_back = at_first(x(2 * half_blocks - j).astype(F32), b_back)
            even, odd = a + b, a - b
            even_back, odd_back = a_back + b_back, a_back - b_back
            odd_sin = odd + odd_back
            if j == 0:
                a_mid = x(quads).astype(F32)
                b_mid = x(half_blocks + quads).astype(F32)
                odd_sin = at_first(a_mid - b_mid, odd_sin)
                mid[...] = (a_mid + b_mid)[:, :1] * alternate
            for i, term in enumerate((even + even_back, even - even_back, odd - odd_back, odd_sin)):
                high = term.astype(BF16)
                lhs[i, :W, j * wide : (j + 1) * wide] = high
                lhs[i, W:, j * wide : (j + 1) * wide] = (term - high.astype(F32)).astype(BF16)

    def transform(h, at):
        def part(i):
            both = dot(lhs[i], table[h, i])
            return both[:W] + both[W:]

        middle = mid[...]
        for parity in range(2):
            re = part(2 * parity)
            im = part(2 * parity + 1)
            if parity == 0:
                re = re + jnp.concatenate([middle, middle], axis=1)
            square = (re * re + im * im).astype(BF16)
            for i in range(2):
                lanes = slice(i * W, (i + 1) * W)
                spec[4 * h + 2 * i + parity, at, :W] = re[:, lanes]
                spec[4 * h + 2 * i + parity, at, W:] = im[:, lanes]
                power[2 * h + i, at, parity * W : (parity + 1) * W] = square[:, lanes]

    def whiten(g, s, factors):
        at = rows_of(s)
        around = jnp.where(
            low_lane,
            power[g + 1, at, :] if g + 1 < groups else jnp.zeros((), BF16),
            power[g - 1, at, :] if g > 0 else jnp.zeros((), BF16),
        )
        parts = [power[g, at, :], around]
        if g + 1 == groups:
            parts.append(near[at, :])
        window = dot(jnp.concatenate(parts, axis=1), band[: len(parts) * wide, :])
        u = g * wide + place(iota((1, wide), 1), fq)
        number = (jnp.minimum(u, HALF) + HALF + 1).astype(F32)
        factor = jnp.concatenate([factors, factors], axis=1) * lax.rsqrt(window / number + EPS)
        for parity in range(2):
            scale = factor[:, parity * W : (parity + 1) * W]
            q = 2 * g + parity
            re = (spec[q, at, :W] * scale).astype(BF16)
            im = (spec[q, at, W:] * scale).astype(BF16)
            if q + LATE < chunks:
                own[q, at, :W] = re
                own[q, at, W:] = im
            else:
                for i in range(BLOCKS):
                    to = pl.ds(pl.multiple_of(s * R, R), R)
                    own_last[i, q + LATE - chunks, to, :W] = re[i * R : (i + 1) * R]
                    own_last[i, q + LATE - chunks, to, W:] = im[i * R : (i + 1) * R]

    def power_copy(s):
        return pltpu.make_async_remote_copy(
            src_ref=power.at[groups - 1, rows_of(s)], dst_ref=near.at[rows_of(s)],
            send_sem=p_send.at[s], recv_sem=p_recv.at[s],
            device_id={"freq": twin}, device_id_type=MESH,
        )

    def white_copy(q, at):
        return pltpu.make_async_remote_copy(
            src_ref=own.at[q, at], dst_ref=recv.at[q, at],
            send_sem=w_send.at[q], recv_sem=w_recv.at[q],
            device_id={"chan": dst}, device_id_type=MESH,
        )

    def last_copy(i):
        return pltpu.make_async_remote_copy(
            src_ref=own_last.at[i], dst_ref=recv_last.at[i],
            send_sem=t_send.at[i], recv_sem=t_recv.at[i],
            device_id={"chan": dst}, device_id_type=MESH,
        )

    def send(q, at):
        @pl.when(has_dst)
        def _():
            white_copy(q, at).start()

    whole = pl.ds(0, rows)

    def rows_of(s):
        return pl.ds(pl.multiple_of(s * W, W), W)

    count_copy = pltpu.make_async_remote_copy(
        src_ref=cnt, dst_ref=crecv, send_sem=c_send, recv_sem=c_recv,
        device_id={"chan": z - 1}, device_id_type=MESH,
    )
    peers = ns + has_dst.astype(jnp.int32) + 2 * ns * sends_h.astype(jnp.int32)

    def segment(s, first):
        at = rows_of(s)
        trace_copy(s).wait()
        fold(at)
        if first:
            table_copy(0).wait()
        transform(0, at)
        whiten_rows = mask[at, :]
        whiten(0, s, whiten_rows)
        if first:
            pl.semaphore_wait(barrier, peers)

            @pl.when(z > 0)
            def _():
                count_copy.start()

        send(0, at)
        send(1, at)
        for h in range(1, groups // 2):
            if first:
                table_copy(h).wait()
            transform(h, at)
        power_copy(s).start()
        whiten(1, s, whiten_rows)
        send(2, at)
        send(3, at)

    segment(0, True)

    def later(s, carry):
        segment(s, False)
        return carry

    lax.fori_loop(1, segs, later, 0)

    def finish(g, s):
        whiten(g, s, mask[rows_of(s), :])

    for g in range(2, groups):
        def each(s, carry, g=g):
            if g + 1 == groups:
                power_copy(s).wait_recv()
            finish(g, s)
            return carry

        lax.fori_loop(0, segs, each, 0)
        for q in (2 * g, 2 * g + 1):
            if q + LATE < chunks:
                send(q, whole)

    @pl.when(has_dst)
    def _():
        for i in range(BLOCKS):
            last_copy(i).start()

    @pl.when(jnp.logical_not(has_src))
    def _():
        def clear(q, carry):
            recv[q] = jnp.zeros((rows, 2 * W), BF16)
            return carry

        lax.fori_loop(0, chunks - LATE, clear, 0)
        recv_last[...] = jnp.zeros_like(recv_last)

    delay_copy.wait()
    total[...] = jnp.zeros_like(total)

    @pl.when(takes_h)
    def _():
        count_copy.wait_recv()

    counts = jnp.concatenate([cnt[...], crecv[...]], axis=1)
    for k in range(slots):
        partner = jnp.where(iota((W, 2 * W), 1) == iota((W, 2 * W), 0) + offs[k], counts, 0).astype(F32)
        fewer = jnp.minimum(cnt_col, jnp.sum(partner, axis=1, keepdims=True))
        inverse[k] = jnp.broadcast_to(1.0 / jnp.maximum(fewer, 1.0), (W, W))

    def below(k, first, number, width):
        return jnp.logical_and(iota((number, width), 0) + (offs[k] + first) >= W, up)

    def products(pieces, chosen, first, number):
        re = [None] * slots
        im = [None] * slots
        for s in range(segs):
            mine, theirs, both = pieces(s)
            pair = dot(chosen, both)
            mine = mine.astype(F32)
            theirs = theirs.astype(F32)
            for k in range(slots):
                other = below(k, first, number, W)
                my_re = jnp.where(other, theirs[:, :W], mine[:, :W])
                my_im = jnp.where(other, theirs[:, W:], mine[:, W:])
                pair_re = pair[k * number : (k + 1) * number, :W]
                pair_im = pair[k * number : (k + 1) * number, W:]
                one = my_re * pair_re + my_im * pair_im
                two = my_im * pair_re - my_re * pair_im
                re[k] = one if s == 0 else re[k] + one
                im[k] = two if s == 0 else im[k] + two
        return [jnp.concatenate([a, b], axis=1).astype(BF16) for a, b in zip(re, im)]

    def correlate(q, carry):
        @pl.when(has_src)
        def _():
            white_copy(q, whole).wait_recv()

        def pieces(s):
            at = slice(s * W, (s + 1) * W)
            mine, theirs = own[q, at, :], recv[q, at, :]
            return mine, theirs, jnp.concatenate([mine, theirs], axis=0)

        for k, cross in enumerate(products(pieces, sel[...], 0, W)):
            total[k] += dot(cross, dly[q])
        return carry

    half = LAGS // 2
    kept = pl.ds(pl.multiple_of(fq * half, half), half)
    given = pl.ds(pl.multiple_of(twin * half, half), half)
    held = BLOCKS // ns
    share = LAGS // ns
    mates = ns // 2

    def share_of(s):
        return pl.ds(pl.multiple_of(lax.rem(s, mates) * share, share), share)

    def hx_copy(i, d):
        peer = lax.rem(s_me + d, ns)
        return pltpu.make_async_remote_copy(
            src_ref=hbuf.at[i, peer // mates, :, :, share_of(peer)],
            dst_ref=hxr.at[i, d - 1], send_sem=hx_send.at[i, d - 1], recv_sem=hx_recv.at[i, d - 1],
            device_id={"seg": peer}, device_id_type=MESH,
        )

    def hz_copy(i, place_in):
        return pltpu.make_async_remote_copy(
            src_ref=hz.at[i],
            dst_ref=hred.at[i % held, :, :, pl.ds(pl.multiple_of(place_in * share, share), share)],
            send_sem=hz_send.at[i], recv_sem=hz_recv.at[i, place_in],
            device_id={"chan": z - 1, "seg": i // held, "freq": s_me // mates}, device_id_type=MESH,
        )

    def hd_copy(i, giver, q):
        return pltpu.make_async_remote_copy(
            src_ref=hbuf.at[i, q],
            dst_ref=hdir.at[i % held, giver], send_sem=hd_send.at[i, q], recv_sem=hd_recv.at[i, giver],
            device_id={"chan": z - 1, "seg": i // held, "freq": q}, device_id_type=MESH,
        )

    def f_copy(i):
        return pltpu.make_async_remote_copy(
            src_ref=fsend.at[i], dst_ref=frecv.at[i], send_sem=f_send.at[i], recv_sem=f_recv.at[i],
            device_id={"freq": twin}, device_id_type=MESH,
        )

    def s_copy(i, slot):
        return pltpu.make_async_remote_copy(
            src_ref=vsum.at[i], dst_ref=srecv.at[i % held, slot],
            send_sem=s_send.at[i], recv_sem=s_recv.at[i, slot],
            device_id={"seg": i // held}, device_id_type=MESH,
        )

    def process(i):
        rows_i = slice(i * R, (i + 1) * R)

        @pl.when(has_src)
        def _():
            last_copy(i).wait_recv()

        chosen = jnp.concatenate([sel[k * W + i * R : k * W + (i + 1) * R, :] for k in range(slots)], axis=0)

        def pieces(p, s):
            at = slice(s * R, (s + 1) * R)
            blocks = [own_last[b, p, at, :] for b in range(BLOCKS)]
            blocks += [recv_last[b, p, at, :] for b in range(i + 1)]
            mine, theirs = blocks[i], blocks[-1]
            blocks += [jnp.zeros((R, 2 * W), BF16)] * (BLOCKS - 1 - i)
            return mine, theirs, jnp.concatenate(blocks, axis=0)

        last = 0.0
        for p in range(LATE):
            cross = jnp.concatenate(products(functools.partial(pieces, p), chosen, i * R, R), axis=0)
            last = last + dot(cross, dly[chunks - LATE + p])
        for k in range(slots):
            sums = total[k, rows_i, :] + last[k * R : (k + 1) * R]
            other = below(k, i * R, R, LAGS)
            returned = jnp.where(other, sums, 0.0).astype(BF16)
            for q in range(2):
                hbuf[i, q, k] = returned[:, q * half : (q + 1) * half]
            total[k, rows_i, :] = jnp.where(other, 0.0, sums)

        for k in range(slots):
            fsend[i, k] = total[k, rows_i, given].astype(BF16)
        f_copy(i).start()

        @pl.when(sends_h)
        def _():
            if i in DIRECT:
                for q in range(2):
                    hd_copy(i, s_me, q).start()
            else:
                for d in range(1, ns):
                    hx_copy(i, d).start()

    def join(i):
        rows_i = slice(i * R, (i + 1) * R)
        f_copy(i).wait_recv()
        for k in range(slots):
            merged = total[k, rows_i, kept] + frecv[i, k].astype(F32)
            total[k, rows_i, kept] = merged
            vsum[i, k] = merged.astype(BF16)

        @pl.when(s_me != i // held)
        def _():
            s_copy(i, lax.rem(s_me - i // held + ns, ns) - 1).start()

    def give_back(i):
        @pl.when(sends_h)
        def _():
            for d in range(1, ns):
                hx_copy(i, d).wait_recv()
            for k in range(slots):
                sums = hbuf[i, s_me // mates, k, :, share_of(s_me)].astype(F32)
                for d in range(1, ns):
                    sums += hxr[i, d - 1, k].astype(F32)
                hz[i, k] = sums.astype(BF16)
            hz_copy(i, lax.rem(s_me, mates)).start()

    lax.fori_loop(0, chunks - LATE, correlate, 0)
    reduced = [i for i in range(BLOCKS) if i not in DIRECT]
    for i in range(BLOCKS):
        process(i)
        if i > 0:
            join(i - 1)
        if i >= LAG and i - LAG in reduced:
            give_back(i - LAG)
    join(BLOCKS - 1)
    for i in reduced:
        if i + LAG >= BLOCKS:
            give_back(i)

    for i in range(BLOCKS):
        rows_i = slice(i * R, (i + 1) * R)
        j = i % held

        @pl.when(s_me == i // held)
        def _():
            for d in range(1, ns):
                s_copy(i, d - 1).wait_recv()

            @pl.when(takes_h)
            def _():
                if i in DIRECT:
                    for e in range(ns):
                        hd_copy(i, e, 0).wait_recv()
                else:
                    for e in range(mates):
                        hz_copy(i, e).wait_recv()

            for k in range(slots):
                result = total[k, rows_i, kept]
                for d in range(1, ns):
                    result += srecv[j, d - 1, k].astype(F32)
                if i in DIRECT:
                    for e in range(ns):
                        result += hdir[j, e, k].astype(F32)
                else:
                    result += hred[j, k].astype(F32)
                scale = inverse[k, rows_i, :]
                out[j * R : (j + 1) * R, k, :] = result * jnp.concatenate([scale] * (half // W), axis=1)

    @pl.when(has_dst)
    def _():
        def drain(q, carry):
            white_copy(q, whole).wait_send()
            return carry

        lax.fori_loop(0, chunks - LATE, drain, 0)
        for i in range(BLOCKS):
            last_copy(i).wait_send()

    @pl.when(z > 0)
    def _():
        count_copy.wait_send()

    @pl.when(sends_h)
    def _():
        for i in range(BLOCKS):
            if i in DIRECT:
                for q in range(2):
                    hd_copy(i, s_me, q).wait_send()
            else:
                for d in range(1, ns):
                    hx_copy(i, d).wait_send()
                hz_copy(i, lax.rem(s_me, mates)).wait_send()

    for s in range(segs):
        power_copy(s).wait_send()
    for i in range(BLOCKS):
        f_copy(i).wait_send()

        @pl.when(s_me != i // held)
        def _():
            s_copy(i, lax.rem(s_me - i // held + ns, ns) - 1).wait_send()


def pin(x):
    return pltpu.with_memory_space_constraint(x, pltpu.HBM)


def shards(traces, dead_mask, seg_counts, offsets):
    segs, chans, length = traces.shape
    nz, ns = lax.axis_size("chan"), lax.axis_size("seg")
    slots = offsets.shape[0]
    chunks = F // 2 // W
    rows = segs * chans
    per = chans // ns
    half = LAGS // 2
    vmem = pl.BlockSpec(memory_space=pltpu.VMEM)
    hbm = pl.BlockSpec(memory_space=pltpu.HBM)
    dma = pltpu.SemaphoreType.DMA
    terms = pl.pallas_call(
        functools.partial(kernel, nz, ns, segs, chunks, slots),
        out_shape=jax.ShapeDtypeStruct((per, slots, half), F32),
        in_specs=[hbm] * 6,
        out_specs=vmem,
        scratch_shapes=[
            pltpu.SMEM((slots,), jnp.int32),
            pltpu.VMEM((1, chans), jnp.int32),
            pltpu.VMEM((1, chans), jnp.int32),
            pltpu.VMEM((rows, length), BF16),
            pltpu.VMEM((1, chans), jnp.int32),
            pltpu.VMEM((slots, W, W), F32),
            pltpu.VMEM((chunks // 4, 4, length // 4, 2 * W), BF16),
            pltpu.VMEM((chunks, 2 * W, LAGS), BF16),
            pltpu.VMEM((4, 2 * W, length // 4), BF16),
            pltpu.VMEM((W, W), F32),
            pltpu.VMEM((6 * W, 2 * W), BF16),
            pltpu.VMEM((chunks, rows, 2 * W), F32),
            pltpu.VMEM((chunks // 2, rows, 2 * W), BF16),
            pltpu.VMEM((rows, 2 * W), BF16),
            pltpu.VMEM((chunks - LATE, rows, 2 * W), BF16),
            pltpu.VMEM((chunks - LATE, rows, 2 * W), BF16),
            pltpu.VMEM((BLOCKS, LATE, segs * R, 2 * W), BF16),
            pltpu.VMEM((BLOCKS, LATE, segs * R, 2 * W), BF16),
            pltpu.VMEM((slots * W, 2 * W), BF16),
            pltpu.VMEM((rows, W), F32),
            pltpu.VMEM((slots, W, LAGS), F32),
            pltpu.VMEM((BLOCKS, 2, slots, R, half), BF16),
            pltpu.VMEM((BLOCKS, ns - 1, slots, R, LAGS // ns), BF16),
            pltpu.VMEM((BLOCKS, slots, R, LAGS // ns), BF16),
            pltpu.VMEM((BLOCKS // ns, slots, R, half), BF16),
            pltpu.VMEM((BLOCKS // ns, ns, slots, R, half), BF16),
            pltpu.VMEM((BLOCKS, slots, R, half), BF16),
            pltpu.VMEM((BLOCKS, slots, R, half), BF16),
            pltpu.VMEM((BLOCKS, slots, R, half), BF16),
            pltpu.VMEM((BLOCKS // ns, ns - 1, slots, R, half), BF16),
            dma((3,)),
            dma((segs,)),
            dma,
            dma,
            dma((chunks // 4,)),
            dma,
            dma((segs,)),
            dma((segs,)),
            dma((chunks - LATE,)),
            dma((chunks - LATE,)),
            dma((BLOCKS,)),
            dma((BLOCKS,)),
            dma((BLOCKS, ns - 1)),
            dma((BLOCKS, ns - 1)),
            dma((BLOCKS,)),
            dma((BLOCKS, ns // 2)),
            dma((BLOCKS, 2)),
            dma((BLOCKS, ns)),
            dma((BLOCKS,)),
            dma((BLOCKS,)),
            dma((BLOCKS,)),
            dma((BLOCKS, ns - 1)),
        ],
        compiler_params=pltpu.CompilerParams(
            collective_id=0, has_side_effects=True, vmem_limit_bytes=50 * 1024 * 1024
        ),
    )(
        pin(offsets),
        pin(traces.reshape(rows, length)),
        pin(dead_mask.reshape(1, chans)),
        pin(seg_counts.reshape(1, chans)),
        jnp.asarray(fourier_blocks(length)),
        jnp.asarray(delay_blocks(length, chunks)),
    )
    return terms


def solution(mesh):
    in_specs = (
        P("seg", ("groups", "chan"), None),
        P(("groups", "chan")),
        P(("groups", "chan")),
        P(),
    )
    out_specs = P(("groups", "chan", "seg"), None, "freq")
    return jax.shard_map(shards, mesh=mesh, in_specs=in_specs, out_specs=out_specs, check_vma=False)
```
